512 devices in a mesh: group: 8 (over y, x_lo), member: 64 (over z, x_hi, core).
Axes of the slice: x: 4 (x_hi: 2, x_lo: 2; x = x_hi * 2 + x_lo), y: 4, z: 16, core: 2. Of those that a mesh axis runs over, the one named last changes fastest.
Arguments:
- student: bfloat16 [196608, 768], P(('group', 'member')), may hold values from -0.29882812 to 0.29882812
- teacher: bfloat16 [196608, 1024], P(('group', 'member')), may hold values from -14 to 14
- counts: int32 [196608], P(('group', 'member')), may hold values from 1 to 7, as said below
- plan: int32 [8, 64, 5], P('group', 'member'), may hold values from 0 to 1, as said below
Outputs:
- grad_student: float32 [196608, 768], P(('group', 'member'))
- loss: float32 [], replicated
The draws below stay inside these ranges and needn't reach their ends.
Inputs may be any that keep to these rules, and one draw needn't show every extreme that they name: `counts`: each row's count is a whole number from 1 up. The pairing is symmetric: plan[g, m, 2 + k - 1] equals plan[g, (m + k) mod 64, k - 1] for k = 1 to 2, and plan[g, m, 4] equals plan[g xor 1, m, 4].
All inputs are finite; a program needn't handle non-finite values.
Results may differ from the reference program's by a relative error of at most 0.0046.
Values may be sent and summed in bfloat16 or wider, within the bound.
A program may use at most 64 MiB of HBM per device.

```python
import jax
import jax.numpy as jnp
from jax import lax

DS = 768
DT = 1024
ROWS_DEV = 384
SPAN = 2
ROWS = 196608
N_GROUP = 8
N_MEMBER = 64


def draw_teacher(key, part):
    base = jnp.clip(jax.random.normal(jax.random.fold_in(key, 11), (ROWS, DT), jnp.float32), -6.0, 6.0)
    shared = jnp.clip(jax.random.normal(jax.random.fold_in(key, 12), (DT,), jnp.float32), -4.0, 4.0)
    position = jnp.arange(ROWS, dtype=jnp.float32) / ROWS
    strength = 0.35 * position
    values = base + strength[:, None] * shared[None, :]
    return jnp.clip(values, -14.0, 14.0).astype(jnp.bfloat16)


def draw_counts(key, part):
    position = jnp.arange(ROWS, dtype=jnp.int32)
    ceiling = 1 + 7 * position // ROWS
    return (1 + jax.random.randint(key, (ROWS,), 0, ceiling)).astype(jnp.int32)


def draw_plan(key, part):
    member_ids = jnp.arange(N_MEMBER, dtype=jnp.int32)
    chance = jnp.where(member_ids < N_MEMBER // 4, 95, 30)
    lower_cols = []
    upper_cols = []
    for offset in range(1, SPAN + 1):
        rolled = jax.random.randint(jax.random.fold_in(key, offset), (N_GROUP, N_MEMBER), 0, 100)
        edge = (rolled < chance[None, :]).astype(jnp.int32)
        upper_cols.append(edge)
        lower_cols.append(jnp.roll(edge, offset, axis=1))
    rolled = jax.random.randint(jax.random.fold_in(key, 977), (N_GROUP // 2, N_MEMBER), 0, 100)
    cross = jnp.repeat((rolled < chance[None, :]).astype(jnp.int32), 2, axis=0)
    return jnp.stack(lower_cols + upper_cols + [cross], axis=-1).astype(jnp.int32)


def block_scale(own_key, extent, shards, smallest, largest):
    loudness = 1.0
    for dim, blocks in shards:
        heights = jax.random.uniform(jax.random.fold_in(jax.random.fold_in(own_key, 6), dim), (blocks,), jnp.float32, smallest / len(shards), largest / len(shards))
        loudness = loudness * jnp.repeat(jnp.exp(heights), extent[dim] // blocks).reshape((-1,) + (1,) * (len(extent) - 1 - dim))
    return loudness


def noise(stream_key, shape, width, reach, split=(), kind=jnp.bfloat16):
    result = jax.random.normal(stream_key, shape, jnp.float32) * width
    if len(split) > 0:
        result = block_scale(stream_key, shape, split, -0.22, 0.18) * result
    return jnp.clip(result, min=-reach, max=reach).astype(kind)


def setup_inputs(seed: int = 0) -> dict:
    arg_keys = jax.random.split(jax.random.key(seed), 5)
    return {
        "student": noise(arg_keys[0], (ROWS, DS), 0.05, 0.29882812, ((0, 512),)),
        "teacher": draw_teacher(jax.random.fold_in(arg_keys[4], 71), 0),
        "counts": draw_counts(jax.random.fold_in(arg_keys[4], 71), 0),
        "plan": draw_plan(jax.random.fold_in(arg_keys[4], 71), 0),
    }


EPS = 1e-06

def normalize(embeddings):
    widened = embeddings.astype(jnp.float32)
    row_scale = lax.rsqrt(lax.optimization_barrier(jnp.sum(widened * widened, axis=-1, keepdims=True)) + EPS)
    return ((widened * row_scale).astype(jnp.bfloat16), row_scale)

def pair_terms(local_s, local_t, local_w, partner_s, partner_t, partner_w, switches):
    highest = lax.Precision.HIGHEST
    student_sim = jnp.einsum('bid,bjd->bij', local_s.astype(jnp.float32), partner_s.astype(jnp.float32), precision=highest)
    teacher_sim = jnp.einsum('bid,bjd->bij', local_t.astype(jnp.float32), partner_t.astype(jnp.float32), precision=highest)
    mismatch = student_sim - teacher_sim
    pair_weight = local_w[:, :, None] * partner_w[:, None, :] * switches[:, None, None]
    rounded = lax.optimization_barrier((pair_weight * mismatch).astype(jnp.bfloat16))
    coefficient = rounded.astype(jnp.float32)
    contrib = jnp.einsum('bij,bjd->bid', coefficient, partner_s.astype(jnp.float32), precision=highest)
    return (contrib, jnp.sum(pair_weight * mismatch * mismatch), jnp.sum(pair_weight))

def reference(student, teacher, counts, plan):
    unit_student, row_scale = normalize(student)
    unit_teacher, unused_scale = normalize(teacher)
    weights = counts.astype(jnp.float32)
    switches = plan.astype(jnp.float32)
    s_blocks = unit_student.reshape(N_GROUP, N_MEMBER, ROWS_DEV, DS)
    t_blocks = unit_teacher.reshape(N_GROUP, N_MEMBER, ROWS_DEV, DT)
    w_blocks = weights.reshape(N_GROUP, N_MEMBER, ROWS_DEV)
    scale_blocks = row_scale.reshape(N_GROUP, N_MEMBER, ROWS_DEV, 1)
    all_on = jnp.ones((N_MEMBER,), jnp.float32)
    loss_sum = jnp.float32(0.0)
    weight_sum = jnp.float32(0.0)
    gradients = []
    for group_index in range(N_GROUP):
        local_rows = (s_blocks[group_index], t_blocks[group_index], w_blocks[group_index])
        summed_grad, loss_part, weight_part = pair_terms(*local_rows, *local_rows, all_on)
        loss_sum = loss_sum + loss_part
        weight_sum = weight_sum + weight_part
        for offset in range(1, SPAN + 1):
            for column, moved in ((offset - 1, offset), (SPAN + offset - 1, -offset)):
                partner = tuple((jnp.roll(array, moved, axis=0) for array in local_rows))
                contrib, loss_part, weight_part = pair_terms(*local_rows, *partner, switches[group_index, :, column])
                summed_grad = summed_grad + contrib
                loss_sum = loss_sum + loss_part
                weight_sum = weight_sum + weight_part
        other = group_index ^ 1
        partner = (s_blocks[other], t_blocks[other], w_blocks[other])
        contrib, loss_part, weight_part = pair_terms(*local_rows, *partner, switches[group_index, :, 2 * SPAN])
        summed_grad = summed_grad + contrib
        loss_sum = loss_sum + loss_part
        weight_sum = weight_sum + weight_part
        unit_float = s_blocks[group_index].astype(jnp.float32)
        along_unit = lax.optimization_barrier(jnp.sum(summed_grad * unit_float, axis=-1, keepdims=True))
        gradients.append(4.0 * scale_blocks[group_index] * (summed_grad - along_unit * unit_float))
    grad_student = jnp.stack(gradients).reshape(ROWS, DS)
    loss = DS * loss_sum / weight_sum
    return (grad_student, loss)
```

```python
import functools

import jax
import jax.numpy as jnp
from jax import lax
from jax.experimental import pallas as pl
from jax.experimental.pallas import tpu as pltpu
from jax.sharding import PartitionSpec as P

EPS = 1e-06
MESH = pl.DeviceIdType.MESH
ROWS = 384
DS = 768
DT = 1024
DU = DS + DT
THIRD = 128
CHUNK = 32
NC = ROWS // CHUNK
F32 = jnp.float32
BF16 = jnp.bfloat16


def kernel(
    n_group, n_member,
    s_hbm, t_hbm, c_ref, plan_ref,
    grad_hbm, loss_ref,
    s_in, t_in, slots, lhs, acc, scale, wcol, wbuf, wrow, lossacc, tiles, out_buf,
    in_sem, send, recv, xsend, xrecv, wsend, wrecv, ar_send, ar_recv, out_sem,
):
    g = lax.axis_index("group")
    m = lax.axis_index("member")
    core = lax.rem(m, 2)
    x_hi = lax.rem(m // 2, 2)
    g_xor = g + 1 - 2 * lax.rem(g, 2)
    m_core = m + 1 - 2 * core
    m_xhi = m + 2 - 4 * x_hi
    m_z = lax.rem(m + 4 - 8 * x_hi + n_member, n_member)
    m_zback = lax.rem(m - 4 + 8 * x_hi + n_member, n_member)
    m_r = lax.rem(m - 2 + 4 * x_hi + n_member, n_member)
    m_f = lax.rem(m - 1 + 2 * core + n_member, n_member)

    def device(group, member):
        return {"group": group, "member": member}

    def rounds(r, d):
        if r == 0:
            base = (m // 8) * 8
            return device(g, base + lax.rem(m - base + d, 8))
        if r == 1:
            return device(lax.rem(g + d, 8), m)
        return device(g, lax.rem(m + 8 * d, n_member))

    copies = []
    for third in range(3):
        rows = pl.ds(third * THIRD, THIRD)
        for which, (src, dst) in enumerate(((s_hbm, s_in), (t_hbm, t_in))):
            copy = pltpu.make_async_copy(src.at[rows], dst.at[rows], in_sem.at[which, third])
            copy.start()
            copies.append(copy)

    barrier = pltpu.get_barrier_semaphore()
    peers = [
        device(g, m_core), device(g_xor, m), device(g, m_xhi), device(g, m_r), device(g, m_f),
        device(g_xor, m_xhi), device(g, m_z), device(g, m_zback),
    ]
    for r in range(3):
        for d in range(1, 8):
            peers.append(rounds(r, d))
    for peer in peers:
        pl.semaphore_signal(barrier, inc=1, device_id=peer, device_id_type=MESH)

    for third in range(3):
        row = c_ref[:, third * THIRD:(third + 1) * THIRD].astype(F32)
        wide = jnp.broadcast_to(row, (THIRD, THIRD))
        wcol[pl.ds(third * THIRD, THIRD), :] = wide.T
        wbuf[0, third] = jnp.broadcast_to(row, (8, THIRD))

    def normalise(k):
        rows = pl.ds(pl.multiple_of(k * CHUNK, CHUNK), CHUNK)
        x = s_in[rows, :].astype(F32)
        rs = lax.rsqrt(jnp.sum(x * x, axis=-1, keepdims=True) + EPS)
        u = (x * rs).astype(BF16)
        slots[0, rows, 0:DS] = u
        lhs[rows, 0:DS] = u
        scale[rows, :] = rs
        y = t_in[rows, :].astype(F32)
        ts = lax.rsqrt(jnp.sum(y * y, axis=-1, keepdims=True) + EPS)
        v = (y * ts).astype(BF16)
        slots[0, rows, DS:DU] = v
        lhs[rows, DS:DU] = -v

    def block_copy(k, src, dst, flow, to):
        rows = pl.ds(pl.multiple_of(k * CHUNK, CHUNK), CHUNK)
        return pltpu.make_async_remote_copy(
            src_ref=slots.at[src, rows], dst_ref=slots.at[dst, rows],
            send_sem=send.at[flow, k], recv_sem=recv.at[flow, k],
            device_id=to, device_id_type=MESH,
        )

    to_p = lambda k: block_copy(k, 0, 2, 0, device(g_xor, m))
    to_q = lambda k: block_copy(k, 2, 3, 1, device(g_xor, m_xhi))
    to_r = lambda k: block_copy(k, 3, 4, 2, device(g, m_z))
    role = lax.rem(x_hi + core, 2)
    to_f = lambda k: block_copy(k, 3 + role, 5, 3, device(g, m_core))

    def to_core(third):
        rows = pl.ds(pl.multiple_of(third * THIRD, THIRD), THIRD)
        return pltpu.make_async_remote_copy(
            src_ref=slots.at[0, rows], dst_ref=slots.at[1, rows],
            send_sem=xsend.at[third], recv_sem=xrecv.at[third],
            device_id=device(g, m_core), device_id_type=MESH,
        )

    per_third = THIRD // CHUNK
    w_peers = [device(g, m_core), device(g_xor, m), device(g, m_xhi), device(g, m_r), device(g, m_f)]
    w_copies = [
        pltpu.make_async_remote_copy(
            src_ref=wbuf.at[0], dst_ref=wbuf.at[slot + 1],
            send_sem=wsend.at[slot], recv_sem=wrecv.at[slot],
            device_id=peer, device_id_type=MESH,
        )
        for slot, peer in enumerate(w_peers)
    ]

    for third in range(3):
        copies[2 * third].wait()
        copies[2 * third + 1].wait()

        @pl.loop(third * per_third, (third + 1) * per_third)
        def _(k):
            normalise(k)

        if third == 0:
            pl.semaphore_wait(barrier, len(peers))

        @pl.loop(third * per_third, (third + 1) * per_third)
        def _(k):
            to_p(k).start()

        to_core(third).start()
        if third == 0:
            for copy in w_copies:
                copy.start()

    acc[...] = jnp.zeros_like(acc)
    lossacc[...] = jnp.zeros_like(lossacc)

    low, high = 0, 2
    columns = [high - 2 * core, 4 + 0 * core, 3 - 2 * x_hi, 1 + 2 * x_hi, 2 * core]
    total_w = jnp.zeros((8, THIRD), F32)
    for third in range(3):
        wrow[0, third] = wbuf[0, third]
        total_w = total_w + wbuf[0, third]
    own_w = jnp.sum(total_w, axis=-1, keepdims=True)
    for slot in range(5):
        w_copies[slot].wait()
        switch = plan_ref[0, 0, columns[slot]].astype(F32)
        for third in range(3):
            w = wbuf[slot + 1, third] * switch
            wrow[slot + 1, third] = w
            total_w = total_w + w
    weight_lanes = total_w * own_w

    def piece(pair, third):
        rows = pl.ds(pl.multiple_of(third * THIRD, THIRD), THIRD)
        both = jnp.concatenate([slots[2 * pair, rows, :], slots[2 * pair + 1, rows, :]], axis=0)
        diff = lax.dot_general(
            lhs[...], both, (((1,), (1,)), ((), ())), preferred_element_type=F32
        )
        w_j = jnp.concatenate([wrow[2 * pair, third], wrow[2 * pair + 1, third]], axis=1)[0:1]
        w_i = wcol[...]
        weighted = jnp.concatenate([w_i, w_i], axis=1) * w_j * diff
        loss = weighted * diff
        lossacc[...] += jnp.sum(loss.reshape(ROWS // 8, 8, 2 * THIRD), axis=0)
        acc[...] += jnp.dot(weighted.astype(BF16), both[:, 0:DS], preferred_element_type=F32)

    @pl.loop(0, NC + 3)
    def _(k):
        @pl.when(k < NC)
        def _():
            to_p(k).wait_recv()
            to_q(k).start()

        @pl.when((k >= 1) & (k <= NC))
        def _():
            to_q(k - 1).wait_recv()
            to_r(k - 1).start()

        @pl.when((k >= 2) & (k <= NC + 1))
        def _():
            to_r(k - 2).wait_recv()
            to_f(k - 2).start()

        @pl.when(k >= 3)
        def _():
            to_f(k - 3).wait_recv()

        @pl.when(k < 3)
        def _():
            to_core(k).wait_recv()

        @pl.when((k < 3) | (lax.rem(k, 2) == 0))
        def _():
            early = jnp.where(k < 3, 1, 0)
            q = jnp.maximum(k - 4, 0)
            pair = (1 - early) * (1 + lax.rem(q // 2, 2))
            third = early * k + (1 - early) * (q // 4)
            piece(pair, third)

    loss_lanes = jnp.sum(lossacc[:, 0:THIRD] + lossacc[:, THIRD:], axis=0, keepdims=True)
    row_id = lax.broadcasted_iota(jnp.int32, (8, THIRD), 0)
    tile = jnp.where(row_id == 0, jnp.broadcast_to(loss_lanes, (8, THIRD)), weight_lanes)
    place = [lax.rem(m, 8), g, m // 8]

    def send_round(r, value):
        tiles[r, place[r]] = value
        for d in range(1, 8):
            pltpu.make_async_remote_copy(
                src_ref=tiles.at[r, place[r]], dst_ref=tiles.at[r, place[r]],
                send_sem=ar_send.at[r], recv_sem=ar_recv.at[r],
                device_id=rounds(r, d), device_id_type=MESH,
            ).start()

    def finish_round(r):
        seven = tiles.at[r, pl.ds(0, 7)]
        pltpu.make_async_copy(seven, seven, ar_recv.at[r]).wait()
        total = tiles[r, 0]
        for d in range(1, 8):
            total = total + tiles[r, d]
        return total

    send_round(0, tile)

    @pl.loop(0, NC)
    def _(k):
        rows = pl.ds(pl.multiple_of(k * CHUNK, CHUNK), CHUNK)
        u = slots[0, rows, 0:DS].astype(F32)
        a = acc[rows, :]
        along = jnp.sum(a * u, axis=-1, keepdims=True)
        out_buf[rows, :] = (4.0 * scale[rows, :]) * (a - along * u)

    out_copy = pltpu.make_async_copy(out_buf, grad_hbm, out_sem)
    out_copy.start()

    tile = finish_round(0)
    send_round(1, tile)
    tile = finish_round(1)
    send_round(2, tile)

    @pl.loop(0, NC)
    def _(k):
        for copy in (to_p, to_q, to_r, to_f):
            copy(k).wait_send()

    for third in range(3):
        to_core(third).wait_send()

    tile = finish_round(2)
    sums = jnp.sum(tile, axis=-1, keepdims=True)
    loss_ref[...] = DS * sums[0:1] / sums[1:2]

    for r in range(3):
        seven = tiles.at[r, pl.ds(0, 7)]
        pltpu.make_async_copy(seven, seven, ar_send.at[r]).wait()
    out_copy.wait()


def per_device(student, teacher, counts, plan):
    n_group = lax.axis_size("group")
    n_member = lax.axis_size("member")
    any_space = pl.BlockSpec(memory_space=pl.ANY)
    vmem = pl.BlockSpec(memory_space=pltpu.VMEM)
    smem = pl.BlockSpec(memory_space=pltpu.SMEM)
    dma = pltpu.SemaphoreType.DMA
    grad, loss = pl.pallas_call(
        functools.partial(kernel, n_group, n_member),
        out_shape=(
            jax.ShapeDtypeStruct((ROWS, DS), F32),
            jax.ShapeDtypeStruct((1, 1), F32),
        ),
        in_specs=[any_space, any_space, vmem, smem],
        out_specs=(any_space, vmem),
        scratch_shapes=[
            pltpu.VMEM((ROWS, DS), BF16),
            pltpu.VMEM((ROWS, DT), BF16),
            pltpu.VMEM((6, ROWS, DU), BF16),
            pltpu.VMEM((ROWS, DU), BF16),
            pltpu.VMEM((ROWS, DS), F32),
            pltpu.VMEM((ROWS, 1), F32),
            pltpu.VMEM((ROWS, THIRD), F32),
            pltpu.VMEM((6, 3, 8, THIRD), F32),
            pltpu.VMEM((6, 3, 8, THIRD), F32),
            pltpu.VMEM((8, 2 * THIRD), F32),
            pltpu.VMEM((3, 8, 8, THIRD), F32),
            pltpu.VMEM((ROWS, DS), F32),
            dma((2, 3)),
            dma((4, NC)),
            dma((4, NC)),
            dma((3,)),
            dma((3,)),
            dma((5,)),
            dma((5,)),
            dma((3,)),
            dma((3,)),
            dma,
        ],
        compiler_params=pltpu.CompilerParams(
            collective_id=0, has_side_effects=True, vmem_limit_bytes=48 * 1024 * 1024
        ),
    )(student, teacher, counts.reshape(1, ROWS), plan)
    return grad, loss.reshape(())


def solution(mesh):
    return jax.shard_map(
        per_device,
        mesh=mesh,
        in_specs=(
            P(("group", "member"), None),
            P(("group", "member"), None),
            P(("group", "member")),
            P("group", "member", None),
        ),
        out_specs=(P(("group", "member"), None), P()),
        check_vma=False,
    )
```

```python
import functools
import itertools

import jax
import jax.numpy as jnp
from jax import lax
from jax.experimental import pallas as pl
from jax.experimental.pallas import tpu as pltpu
from jax.sharding import PartitionSpec as P

EPS = 1e-06
MESH = pl.DeviceIdType.MESH
ROWS = 384
DS = 768
DT = 1024
DU = DS + DT
THIRD = 128
CHUNK = 16
NC = ROWS // CHUNK
PER_THIRD = NC // 3
LAG_Q, LAG_R, LAG_F = 3, 6, 8
STEPS = NC + LAG_F
EARLY = 3
TOKENS = 8
NORM = 32
F32 = jnp.float32
BF16 = jnp.bfloat16


def kernel(
    n_group, n_member,
    s_hbm, t_hbm, c_hbm, plan_hbm,
    grad_hbm, loss_ref,
    s_in, t_in, c_in, plan_in, switches, slots, lhs, acc, scale, wcol, wbuf, lossacc, tiles, out_buf,
    in_sem, send, recv, xsend, xrecv, wsend, wrecv, ar_send, ar_recv, out_sem, tokens,
):
    g = lax.axis_index("group")
    m = lax.axis_index("member")
    core = lax.rem(m, 2)
    x_hi = lax.rem(m // 2, 2)
    x_lo = lax.rem(g, 2)
    g_xor = g + 1 - 2 * x_lo
    m_core = m + 1 - 2 * core
    m_xhi = m + 2 - 4 * x_hi
    m_up = lax.rem(m + 4, n_member)
    m_down = lax.rem(m - 4 + n_member, n_member)
    m_z = lax.rem(m + 4 - 8 * x_hi + n_member, n_member)
    g_up = lax.rem(g + 2, n_group)
    g_down = lax.rem(g - 2 + n_group, n_group)
    role = lax.rem(x_hi + core, 2)

    def device(group, member):
        return {"group": group, "member": member}

    small = [
        pltpu.make_async_copy(c_hbm, c_in, in_sem.at[2, 0]),
        pltpu.make_async_copy(plan_hbm, plan_in, in_sem.at[2, 1]),
    ]
    copies = []
    for third in range(3):
        rows = pl.ds(third * THIRD, THIRD)
        for which, (src, dst) in enumerate(((s_hbm, s_in), (t_hbm, t_in))):
            copies.append(pltpu.make_async_copy(src.at[rows], dst.at[rows], in_sem.at[which, third]))
    for copy in copies[:2] + small + copies[2:]:
        copy.start()

    barrier = pltpu.get_barrier_semaphore()
    xor_peer = device(g_xor, m)
    x_other = device(g_xor, m_xhi)
    sides = [
        (xor_peer, 0), (x_other, 1),
        (device(g, m_up), 3), (device(g, m_down), 2),
        (device(g_up, m), 5), (device(g_down, m), 4),
    ]
    near = [peer for peer, _ in sides] + [device(g, m_core)]
    for peer in near:
        pl.semaphore_signal(barrier, inc=1, device_id=peer, device_id_type=MESH)

    def normalise(k):
        rows = pl.ds(pl.multiple_of(k * NORM, NORM), NORM)
        x = s_in[rows, :].astype(F32)
        rs = lax.rsqrt(jnp.sum(x * x, axis=-1, keepdims=True) + EPS)
        u = (x * rs).astype(BF16)
        slots[0, rows, 0:DS] = u
        lhs[rows, 0:DS] = u
        scale[rows, :] = rs
        y = t_in[rows, :].astype(F32)
        ts = lax.rsqrt(jnp.sum(y * y, axis=-1, keepdims=True) + EPS)
        v = (y * ts).astype(BF16)
        slots[0, rows, DS:DU] = v
        lhs[rows, DS:DU] = -v

    flows = [
        (0, 2, xor_peer), (2, 3, x_other), (3, 4, device(g, m_z)), (3 + role, 5, device(g, m_core)),
    ]

    def block_copy(flow, k):
        src, dst, to = flows[flow]
        rows = pl.ds(pl.multiple_of(k * CHUNK, CHUNK), CHUNK)
        return pltpu.make_async_remote_copy(
            src_ref=slots.at[src, rows], dst_ref=slots.at[dst, rows],
            send_sem=send.at[flow, k], recv_sem=recv.at[flow, k],
            device_id=to, device_id_type=MESH,
        )

    def w_copy(flow):
        src, dst, to = (flows + [(0, 1, device(g, m_core))])[flow]
        return pltpu.make_async_remote_copy(
            src_ref=wbuf.at[src], dst_ref=wbuf.at[dst],
            send_sem=wsend.at[flow], recv_sem=wrecv.at[flow],
            device_id=to, device_id_type=MESH,
        )

    def to_core(third):
        rows = pl.ds(pl.multiple_of(third * THIRD, THIRD), THIRD)
        return pltpu.make_async_remote_copy(
            src_ref=slots.at[0, rows], dst_ref=slots.at[1, rows],
            send_sem=xsend.at[third], recv_sem=xrecv.at[third],
            device_id=device(g, m_core), device_id_type=MESH,
        )

    for third in range(3):
        copies[2 * third].wait()
        copies[2 * third + 1].wait()

        @pl.loop(third * (THIRD // NORM), (third + 1) * (THIRD // NORM))
        def _(k):
            normalise(k)

        if third == 0:
            for copy in small:
                copy.wait()
            for part in range(3):
                row = c_in[pl.ds(part * THIRD, THIRD)].astype(F32).reshape(1, THIRD)
                wide = jnp.broadcast_to(row, (THIRD, THIRD))
                wcol[pl.ds(part * THIRD, THIRD), :] = wide.T
                wbuf[0, part] = jnp.broadcast_to(row, (8, THIRD))
            pl.semaphore_wait(barrier, len(near))

        @pl.loop(third * PER_THIRD, (third + 1) * PER_THIRD)
        def _(k):
            block_copy(0, k).start()

        to_core(third).start()
        if third == 0:
            w_copy(0).start()
            w_copy(4).start()

    acc[...] = jnp.zeros_like(acc)
    lossacc[...] = jnp.zeros_like(lossacc)

    columns = [2 - 2 * core, 4 + 0 * core, 3 - 2 * x_hi, 1 + 2 * x_hi, 2 * core]
    switches[0] = jnp.float32(1.0)
    for slot in range(5):
        switches[slot + 1] = plan_in[0, 0, columns[slot]].astype(F32)
    w_copy(4).wait_recv()

    def piece(pair, third):
        rows = pl.ds(pl.multiple_of(third * THIRD, THIRD), THIRD)
        both = jnp.concatenate([slots[2 * pair, rows, :], slots[2 * pair + 1, rows, :]], axis=0)
        diff = lax.dot_general(
            lhs[...], both, (((1,), (1,)), ((), ())), preferred_element_type=F32
        )
        w_j = jnp.concatenate(
            [wbuf[2 * pair + b, third] * switches[2 * pair + b] for b in range(2)], axis=1
        )[0:1]
        w_i = wcol[...]
        weighted = jnp.concatenate([w_i, w_i], axis=1) * w_j * diff
        loss = weighted * diff
        lossacc[...] += jnp.sum(loss.reshape(ROWS // 8, 8, 2 * THIRD), axis=0)
        acc[...] += jnp.dot(weighted.astype(BF16), both[:, 0:DS], preferred_element_type=F32)

    def signal_sides():
        for peer, place in sides:
            pl.semaphore_signal(tokens.at[place], inc=1, device_id=peer, device_id_type=MESH)

    def wait_sides():
        for place in range(6):
            pl.semaphore_wait(tokens.at[place], 1)

    @pl.loop(0, STEPS)
    def _(k):
        @pl.when(k < NC)
        def _():
            block_copy(0, k).wait_recv()
            block_copy(1, k).start()

        for flow, lag in ((1, LAG_Q), (2, LAG_R)):
            @pl.when((k >= lag) & (k < NC + lag))
            def _():
                block_copy(flow, k - lag).wait_recv()
                block_copy(flow + 1, k - lag).start()

        @pl.when(k >= LAG_F)
        def _():
            block_copy(3, k - LAG_F).wait_recv()

        for flow, lag in enumerate((0, LAG_Q, LAG_R, LAG_F)):
            @pl.when(k == lag)
            def _():
                w_copy(flow).wait_recv()
                if flow < 3:
                    w_copy(flow + 1).start()

        @pl.when((k >= 2) & (k < 2 + TOKENS))
        def _():
            signal_sides()

        @pl.when((k >= 4) & (k < 4 + TOKENS))
        def _():
            wait_sides()

        @pl.when((k < 2 * EARLY) & (lax.rem(k, 2) == 0))
        def _():
            to_core(k // 2).wait_recv()
            piece(0, k // 2)

        ready = (LAG_Q + PER_THIRD - 1, LAG_F + PER_THIRD - 1)
        for pair in range(2):
            late = k - ready[pair]

            @pl.when((late >= 0) & (lax.rem(late + 3 * NC, PER_THIRD) == 0) & (late < NC))
            def _():
                piece(1 + pair, late // PER_THIRD)

    total_w = jnp.zeros((8, THIRD), F32)
    own_w = jnp.zeros((8, THIRD), F32)
    for third in range(3):
        own_w = own_w + wbuf[0, third]
        for slot in range(6):
            total_w = total_w + wbuf[slot, third] * switches[slot]
    weight_lanes = total_w * jnp.sum(own_w, axis=-1, keepdims=True)
    loss_lanes = jnp.sum(lossacc[:, 0:THIRD] + lossacc[:, THIRD:], axis=0, keepdims=True)
    row_id = lax.broadcasted_iota(jnp.int32, (8, THIRD), 0)
    tile = jnp.where(row_id == 0, jnp.broadcast_to(loss_lanes, (8, THIRD)), weight_lanes)

    y = g // 2
    z = m // 4
    n_y, n_z = n_group // 2, n_member // 4

    def plane_peer(dh, dl, dy):
        member = m + 2 * (lax.rem(x_hi + dh, 2) - x_hi)
        group = g + (lax.rem(x_lo + dl, 2) - x_lo) + 2 * (lax.rem(y + dy, n_y) - y)
        return device(group, member)

    def around(d, n):
        return min(d, n - d)

    plane = sorted(
        (o for o in itertools.product(range(2), range(2), range(n_y)) if any(o)),
        key=lambda o: (-(2 * o[0] + o[1] - 2 * o[0] * o[1] + around(o[2], n_y)), o),
    )
    ring = sorted(range(1, n_z), key=lambda d: (-around(d, n_z), d))
    rounds = [
        (core, [device(g, m_core)]),
        ((x_hi * 2 + x_lo) * n_y + y, [plane_peer(*o) for o in plane]),
        (z, [device(g, lax.rem(m + 4 * d, n_member)) for d in ring]),
    ]

    def send_round(r, value):
        place, peers = rounds[r]
        tiles[r, place] = value
        for peer in peers:
            pltpu.make_async_remote_copy(
                src_ref=tiles.at[r, place], dst_ref=tiles.at[r, place],
                send_sem=ar_send.at[r], recv_sem=ar_recv.at[r],
                device_id=peer, device_id_type=MESH,
            ).start()

    def all_of(r, sems):
        seen = tiles.at[r, pl.ds(0, len(rounds[r][1]))]
        return pltpu.make_async_copy(seen, seen, sems.at[r])

    def finish_round(r):
        all_of(r, ar_recv).wait()
        total = tiles[r, 0]
        for d in range(1, len(rounds[r][1]) + 1):
            total = total + tiles[r, d]
        return total

    send_round(0, tile)
    tile = finish_round(0)
    send_round(1, tile)

    @pl.loop(0, ROWS // NORM)
    def _(k):
        rows = pl.ds(pl.multiple_of(k * NORM, NORM), NORM)
        u = slots[0, rows, 0:DS].astype(F32)
        a = acc[rows, :]
        along = jnp.sum(a * u, axis=-1, keepdims=True)
        out_buf[rows, :] = (4.0 * scale[rows, :]) * (a - along * u)

    out_copy = pltpu.make_async_copy(out_buf, grad_hbm, out_sem)
    out_copy.start()

    tile = finish_round(1)
    send_round(2, tile)

    @pl.loop(0, NC)
    def _(k):
        for flow in range(4):
            block_copy(flow, k).wait_send()

    for third in range(3):
        to_core(third).wait_send()
    for flow in range(5):
        w_copy(flow).wait_send()
    for r in range(2):
        all_of(r, ar_send).wait()
    out_copy.wait()

    tile = finish_round(2)
    sums = jnp.sum(tile, axis=-1, keepdims=True)
    loss_ref[...] = DS * sums[0:1] / sums[1:2]
    all_of(2, ar_send).wait()


def per_device(student, teacher, counts, plan):
    n_group = lax.axis_size("group")
    n_member = lax.axis_size("member")
    any_space = pl.BlockSpec(memory_space=pl.ANY)
    hbm = pl.BlockSpec(memory_space=pltpu.HBM)
    vmem = pl.BlockSpec(memory_space=pltpu.VMEM)
    dma = pltpu.SemaphoreType.DMA
    grad, loss = pl.pallas_call(
        functools.partial(kernel, n_group, n_member),
        out_shape=(
            jax.ShapeDtypeStruct((ROWS, DS), F32),
            jax.ShapeDtypeStruct((1, 1), F32),
        ),
        in_specs=[hbm, hbm, hbm, hbm],
        out_specs=(any_space, vmem),
        scratch_shapes=[
            pltpu.VMEM((ROWS, DS), BF16),
            pltpu.VMEM((ROWS, DT), BF16),
            pltpu.VMEM((ROWS,), jnp.int32),
            pltpu.SMEM((1, 1, 5), jnp.int32),
            pltpu.SMEM((6,), F32),
            pltpu.VMEM((6, ROWS, DU), BF16),
            pltpu.VMEM((ROWS, DU), BF16),
            pltpu.VMEM((ROWS, DS), F32),
            pltpu.VMEM((ROWS, 1), F32),
            pltpu.VMEM((ROWS, THIRD), F32),
            pltpu.VMEM((6, 3, 8, THIRD), F32),
            pltpu.VMEM((8, 2 * THIRD), F32),
            pltpu.VMEM((3, 16, 8, THIRD), F32),
            pltpu.VMEM((ROWS, DS), F32),
            dma((3, 3)),
            dma((4, NC)),
            dma((4, NC)),
            dma((3,)),
            dma((3,)),
            dma((5,)),
            dma((5,)),
            dma((3,)),
            dma((3,)),
            dma,
            pltpu.SemaphoreType.REGULAR((6,)),
        ],
        compiler_params=pltpu.CompilerParams(
            collective_id=0, has_side_effects=True, vmem_limit_bytes=62 * 1024 * 1024
        ),
    )(student, teacher, counts, plan)
    return grad, loss.reshape(())


def solution(mesh):
    return jax.shard_map(
        per_device,
        mesh=mesh,
        in_specs=(
            P(("group", "member"), None),
            P(("group", "member"), None),
            P(("group", "member")),
            P("group", "member", None),
        ),
        out_specs=(P(("group", "member"), None), P()),
        check_vma=False,
    )
```

```python
import functools
import itertools

import jax
import jax.numpy as jnp
from jax import lax
from jax.experimental import pallas as pl
from jax.experimental.pallas import tpu as pltpu
from jax.sharding import PartitionSpec as P

EPS = 1e-06
MESH = pl.DeviceIdType.MESH
ROWS = 384
DS = 768
DT = 1024
DU = DS + DT
THIRD = 128
CHUNK = 16
NC = ROWS // CHUNK
PER_THIRD = NC // 3
LAG_Q, LAG_R, LAG_F = 3, 6, 8
STEPS = NC + LAG_F
EARLY = 3
TOKENS = 8
NORM = 32
F32 = jnp.float32
BF16 = jnp.bfloat16


def kernel(
    n_group, n_member,
    s_hbm, t_hbm, c_hbm, plan_hbm,
    grad_hbm, loss_ref,
    s_in, t_in, c_in, plan_in, switches, slots, lhs, acc, scale, wcol, wbuf, lossacc, tiles, out_buf,
    in_sem, send, recv, xsend, xrecv, wsend, wrecv, ar_send, ar_recv, out_sem, tokens,
):
    g = lax.axis_index("group")
    m = lax.axis_index("member")
    core = lax.rem(m, 2)
    x_hi = lax.rem(m // 2, 2)
    x_lo = lax.rem(g, 2)
    g_xor = g + 1 - 2 * x_lo
    m_core = m + 1 - 2 * core
    m_xhi = m + 2 - 4 * x_hi
    m_up = lax.rem(m + 4, n_member)
    m_down = lax.rem(m - 4 + n_member, n_member)
    m_z = lax.rem(m + 4 - 8 * x_hi + n_member, n_member)
    g_up = lax.rem(g + 2, n_group)
    g_down = lax.rem(g - 2 + n_group, n_group)
    role = lax.rem(x_hi + core, 2)

    def device(group, member):
        return {"group": group, "member": member}

    small = [
        pltpu.make_async_copy(c_hbm, c_in, in_sem.at[2, 0]),
        pltpu.make_async_copy(plan_hbm, plan_in, in_sem.at[2, 1]),
    ]
    copies = []
    for third in range(3):
        rows = pl.ds(third * THIRD, THIRD)
        for which, (src, dst) in enumerate(((s_hbm, s_in), (t_hbm, t_in))):
            copies.append(pltpu.make_async_copy(src.at[rows], dst.at[rows], in_sem.at[which, third]))
    for copy in copies[:2] + small + copies[2:]:
        copy.start()

    barrier = pltpu.get_barrier_semaphore()
    xor_peer = device(g_xor, m)
    x_other = device(g_xor, m_xhi)
    sides = [
        (xor_peer, 0), (x_other, 1),
        (device(g, m_up), 3), (device(g, m_down), 2),
        (device(g_up, m), 5), (device(g_down, m), 4),
    ]
    near = [peer for peer, _ in sides] + [device(g, m_core)]
    for peer in near:
        pl.semaphore_signal(barrier, inc=1, device_id=peer, device_id_type=MESH)

    def normalise(k):
        rows = pl.ds(pl.multiple_of(k * NORM, NORM), NORM)
        x = s_in[rows, :].astype(F32)
        rs = lax.rsqrt(jnp.sum(x * x, axis=-1, keepdims=True) + EPS)
        u = (x * rs).astype(BF16)
        slots[0, rows, 0:DS] = u
        lhs[rows, 0:DS] = u
        scale[rows, :] = rs
        y = t_in[rows, :].astype(F32)
        ts = lax.rsqrt(jnp.sum(y * y, axis=-1, keepdims=True) + EPS)
        v = (y * ts).astype(BF16)
        slots[0, rows, DS:DU] = v
        lhs[rows, DS:DU] = -v

    flows = [
        (0, 2, xor_peer), (2, 3, x_other), (3, 4, device(g, m_z)), (3 + role, 5, device(g, m_core)),
    ]

    def block_copy(flow, k):
        src, dst, to = flows[flow]
        rows = pl.ds(pl.multiple_of(k * CHUNK, CHUNK), CHUNK)
        return pltpu.make_async_remote_copy(
            src_ref=slots.at[src, rows], dst_ref=slots.at[dst, rows],
            send_sem=send.at[flow, k], recv_sem=recv.at[flow, k],
            device_id=to, device_id_type=MESH,
        )

    def w_copy(flow):
        src, dst, to = (flows + [(0, 1, device(g, m_core))])[flow]
        return pltpu.make_async_remote_copy(
            src_ref=wbuf.at[src], dst_ref=wbuf.at[dst],
            send_sem=wsend.at[flow], recv_sem=wrecv.at[flow],
            device_id=to, device_id_type=MESH,
        )

    def to_core(third):
        rows = pl.ds(pl.multiple_of(third * THIRD, THIRD), THIRD)
        return pltpu.make_async_remote_copy(
            src_ref=slots.at[0, rows], dst_ref=slots.at[1, rows],
            send_sem=xsend.at[third], recv_sem=xrecv.at[third],
            device_id=device(g, m_core), device_id_type=MESH,
        )

    for third in range(3):
        copies[2 * third].wait()
        copies[2 * third + 1].wait()

        @pl.loop(third * (THIRD // NORM), (third + 1) * (THIRD // NORM))
        def _(k):
            normalise(k)

        if third == 0:
            for copy in small:
                copy.wait()
            for part in range(3):
                row = c_in[pl.ds(part * THIRD, THIRD)].astype(F32).reshape(1, THIRD)
                wide = jnp.broadcast_to(row, (THIRD, THIRD))
                wcol[pl.ds(part * THIRD, THIRD), :] = wide.T
                wbuf[0, part] = jnp.broadcast_to(row, (8, THIRD))
            pl.semaphore_wait(barrier, len(near))
            w_copy(0).start()
            w_copy(4).start()

        @pl.loop(third * PER_THIRD, (third + 1) * PER_THIRD)
        def _(k):
            block_copy(0, k).start()

        to_core(third).start()

    acc[...] = jnp.zeros_like(acc)
    lossacc[...] = jnp.zeros_like(lossacc)

    columns = [2 - 2 * core, 4 + 0 * core, 3 - 2 * x_hi, 1 + 2 * x_hi, 2 * core]
    switches[0] = jnp.float32(1.0)
    for slot in range(5):
        switches[slot + 1] = plan_in[0, 0, columns[slot]].astype(F32)
    w_copy(4).wait_recv()

    def piece(pair, third):
        rows = pl.ds(pl.multiple_of(third * THIRD, THIRD), THIRD)
        both = jnp.concatenate([slots[2 * pair, rows, :], slots[2 * pair + 1, rows, :]], axis=0)
        diff = lax.dot_general(
            lhs[...], both, (((1,), (1,)), ((), ())), preferred_element_type=F32
        )
        w_j = jnp.concatenate(
            [wbuf[2 * pair + b, third] * switches[2 * pair + b] for b in range(2)], axis=1
        )[0:1]
        w_i = wcol[...]
        weighted = jnp.concatenate([w_i, w_i], axis=1) * w_j * diff
        loss = weighted * diff
        lossacc[...] += jnp.sum(loss.reshape(ROWS // 8, 8, 2 * THIRD), axis=0)
        acc[...] += jnp.dot(weighted.astype(BF16), both[:, 0:DS], preferred_element_type=F32)

    def signal_sides():
        for peer, place in sides:
            pl.semaphore_signal(tokens.at[place], inc=1, device_id=peer, device_id_type=MESH)

    def wait_sides():
        for place in range(6):
            pl.semaphore_wait(tokens.at[place], 1)

    @pl.loop(0, STEPS)
    def _(k):
        @pl.when(k < NC)
        def _():
            block_copy(0, k).wait_recv()
            block_copy(1, k).start()

        for flow, lag in ((1, LAG_Q), (2, LAG_R)):
            @pl.when((k >= lag) & (k < NC + lag))
            def _():
                block_copy(flow, k - lag).wait_recv()
                block_copy(flow + 1, k - lag).start()

        @pl.when(k >= LAG_F)
        def _():
            block_copy(3, k - LAG_F).wait_recv()

        for flow, lag in enumerate((0, LAG_Q, LAG_R, LAG_F)):
            @pl.when(k == lag)
            def _():
                w_copy(flow).wait_recv()
                if flow < 3:
                    w_copy(flow + 1).start()

        @pl.when((k >= 2) & (k < 2 + TOKENS))
        def _():
            signal_sides()

        @pl.when((k >= 4) & (k < 4 + TOKENS))
        def _():
            wait_sides()

        @pl.when((k < 2 * EARLY) & (lax.rem(k, 2) == 0))
        def _():
            to_core(k // 2).wait_recv()
            piece(0, k // 2)

        ready = (LAG_Q + PER_THIRD - 1, LAG_F + PER_THIRD - 1)
        for pair in range(2):
            late = k - ready[pair]

            @pl.when((late >= 0) & (lax.rem(late + 3 * NC, PER_THIRD) == 0) & (late < NC))
            def _():
                piece(1 + pair, late // PER_THIRD)

    total_w = jnp.zeros((8, THIRD), F32)
    own_w = jnp.zeros((8, THIRD), F32)
    for third in range(3):
        own_w = own_w + wbuf[0, third]
        for slot in range(6):
            total_w = total_w + wbuf[slot, third] * switches[slot]
    weight_lanes = total_w * jnp.sum(own_w, axis=-1, keepdims=True)
    loss_lanes = jnp.sum(lossacc[:, 0:THIRD] + lossacc[:, THIRD:], axis=0, keepdims=True)
    row_id = lax.broadcasted_iota(jnp.int32, (8, THIRD), 0)
    tile = jnp.where(row_id == 0, jnp.broadcast_to(loss_lanes, (8, THIRD)), weight_lanes)

    y = g // 2
    z = m // 4
    n_y, n_z = n_group // 2, n_member // 4

    def plane_peer(dh, dl, dy):
        member = m + 2 * (lax.rem(x_hi + dh, 2) - x_hi)
        group = g + (lax.rem(x_lo + dl, 2) - x_lo) + 2 * (lax.rem(y + dy, n_y) - y)
        return device(group, member)

    def around(d, n):
        return min(d, n - d)

    plane = sorted(
        (o for o in itertools.product(range(2), range(2), range(n_y)) if any(o)),
        key=lambda o: (-(2 * o[0] + o[1] - 2 * o[0] * o[1] + around(o[2], n_y)), o),
    )
    ring = sorted(range(1, n_z), key=lambda d: (-around(d, n_z), d))
    rounds = [
        (core, [device(g, m_core)]),
        ((x_hi * 2 + x_lo) * n_y + y, [plane_peer(*o) for o in plane]),
        (z, [device(g, lax.rem(m + 4 * d, n_member)) for d in ring]),
    ]

    def send_round(r, value):
        place, peers = rounds[r]
        tiles[r, place] = value
        for peer in peers:
            pltpu.make_async_remote_copy(
                src_ref=tiles.at[r, place], dst_ref=tiles.at[r, place],
                send_sem=ar_send.at[r], recv_sem=ar_recv.at[r],
                device_id=peer, device_id_type=MESH,
            ).start()

    def all_of(r, sems):
        seen = tiles.at[r, pl.ds(0, len(rounds[r][1]))]
        return pltpu.make_async_copy(seen, seen, sems.at[r])

    def finish_round(r):
        all_of(r, ar_recv).wait()
        total = tiles[r, 0]
        for d in range(1, len(rounds[r][1]) + 1):
            total = total + tiles[r, d]
        return total

    send_round(0, tile)
    tile = finish_round(0)
    send_round(1, tile)

    @pl.loop(0, ROWS // NORM)
    def _(k):
        rows = pl.ds(pl.multiple_of(k * NORM, NORM), NORM)
        u = slots[0, rows, 0:DS].astype(F32)
        a = acc[rows, :]
        along = jnp.sum(a * u, axis=-1, keepdims=True)
        out_buf[rows, :] = (4.0 * scale[rows, :]) * (a - along * u)

    out_copy = pltpu.make_async_copy(out_buf, grad_hbm, out_sem)
    out_copy.start()

    tile = finish_round(1)
    send_round(2, tile)

    @pl.loop(0, NC)
    def _(k):
        for flow in range(4):
            block_copy(flow, k).wait_send()

    for third in range(3):
        to_core(third).wait_send()
    for flow in range(5):
        w_copy(flow).wait_send()
    for r in range(2):
        all_of(r, ar_send).wait()
    out_copy.wait()

    tile = finish_round(2)
    sums = jnp.sum(tile, axis=-1, keepdims=True)
    loss_ref[...] = DS * sums[0:1] / sums[1:2]
    all_of(2, ar_send).wait()


def per_device(student, teacher, counts, plan):
    n_group = lax.axis_size("group")
    n_member = lax.axis_size("member")
    any_space = pl.BlockSpec(memory_space=pl.ANY)
    hbm = pl.BlockSpec(memory_space=pltpu.HBM)
    vmem = pl.BlockSpec(memory_space=pltpu.VMEM)
    dma = pltpu.SemaphoreType.DMA
    grad, loss = pl.pallas_call(
        functools.partial(kernel, n_group, n_member),
        out_shape=(
            jax.ShapeDtypeStruct((ROWS, DS), F32),
            jax.ShapeDtypeStruct((1, 1), F32),
        ),
        in_specs=[hbm, hbm, hbm, hbm],
        out_specs=(any_space, vmem),
        scratch_shapes=[
            pltpu.VMEM((ROWS, DS), BF16),
            pltpu.VMEM((ROWS, DT), BF16),
            pltpu.VMEM((ROWS,), jnp.int32),
            pltpu.SMEM((1, 1, 5), jnp.int32),
            pltpu.SMEM((6,), F32),
            pltpu.VMEM((6, ROWS, DU), BF16),
            pltpu.VMEM((ROWS, DU), BF16),
            pltpu.VMEM((ROWS, DS), F32),
            pltpu.VMEM((ROWS, 1), F32),
            pltpu.VMEM((ROWS, THIRD), F32),
            pltpu.VMEM((6, 3, 8, THIRD), F32),
            pltpu.VMEM((8, 2 * THIRD), F32),
            pltpu.VMEM((3, 16, 8, THIRD), F32),
            pltpu.VMEM((ROWS, DS), F32),
            dma((3, 3)),
            dma((4, NC)),
            dma((4, NC)),
            dma((3,)),
            dma((3,)),
            dma((5,)),
            dma((5,)),
            dma((3,)),
            dma((3,)),
            dma,
            pltpu.SemaphoreType.REGULAR((6,)),
        ],
        compiler_params=pltpu.CompilerParams(
            collective_id=0, has_side_effects=True, vmem_limit_bytes=48 * 1024 * 1024
        ),
    )(*(pltpu.with_memory_space_constraint(a, pltpu.HBM) for a in (student, teacher, counts, plan)))
    return grad, loss.reshape(())


def solution(mesh):
    return jax.shard_map(
        per_device,
        mesh=mesh,
        in_specs=(
            P(("group", "member"), None),
            P(("group", "member"), None),
            P(("group", "member")),
            P("group", "member", None),
        ),
        out_specs=(P(("group", "member"), None), P()),
        check_vma=False,
    )
```

```python
import functools
import itertools

import jax
import jax.numpy as jnp
from jax import lax
from jax.experimental import pallas as pl
from jax.experimental.pallas import tpu as pltpu
from jax.sharding import PartitionSpec as P

EPS = 1e-06
MESH = pl.DeviceIdType.MESH
ROWS = 384
DS = 768
DT = 1024
DU = DS + DT
THIRD = 128
CHUNK = 16
SHORT = 8
HEAD = 0
EXTRA = HEAD - HEAD * SHORT // CHUNK
NC = ROWS // CHUNK + EXTRA
PER_THIRD = THIRD // CHUNK
FIRST = NC - 2 * PER_THIRD
LAG_Q, LAG_R, LAG_F = 4, 8, 10
STEPS = NC + LAG_F
EARLY = 3
LOSS_STEP = LAG_Q + NC - 1
TOKENS = 8
NORM = 32
PARTS = ((0, NORM), (NORM, THIRD), (THIRD, 2 * THIRD), (2 * THIRD, ROWS))
F32 = jnp.float32
BF16 = jnp.bfloat16


def kernel(
    n_group, n_member,
    s_hbm, t_hbm, c_hbm, plan_hbm,
    grad_hbm, loss_ref,
    s_in, t_in, c_in, plan_in, switches, slots, lhs, acc, coef, scale, wcol, mixcol, wbuf, lossacc, tiles, out_buf,
    in_sem, send, recv, xsend, xrecv, nsend, nrecv, wsend, wrecv, ar_send, ar_recv, out_sem, tokens,
):
    g = lax.axis_index("group")
    m = lax.axis_index("member")
    core = lax.rem(m, 2)
    x_hi = lax.rem(m // 2, 2)
    x_lo = lax.rem(g, 2)
    g_xor = g + 1 - 2 * x_lo
    m_core = m + 1 - 2 * core
    m_xhi = m + 2 - 4 * x_hi
    m_up = lax.rem(m + 4, n_member)
    m_down = lax.rem(m - 4 + n_member, n_member)
    m_z = lax.rem(m + 4 - 8 * x_hi + n_member, n_member)
    g_up = lax.rem(g + 2, n_group)
    g_down = lax.rem(g - 2 + n_group, n_group)
    role = lax.rem(x_hi + core, 2)

    def device(group, member):
        return {"group": group, "member": member}

    small = [
        pltpu.make_async_copy(c_hbm, c_in, in_sem.at[2, 0]),
        pltpu.make_async_copy(plan_hbm, plan_in, in_sem.at[2, 1]),
    ]
    copies = []
    for part, (low, high) in enumerate(PARTS):
        rows = pl.ds(low, high - low)
        for which, (src, dst) in enumerate(((s_hbm, s_in), (t_hbm, t_in))):
            copies.append(pltpu.make_async_copy(src.at[rows], dst.at[rows], in_sem.at[which, part]))
    for copy in copies[:2] + small + copies[2:]:
        copy.start()

    barrier = pltpu.get_barrier_semaphore()
    xor_peer = device(g_xor, m)
    x_other = device(g_xor, m_xhi)
    sides = [
        (xor_peer, 0), (x_other, 1),
        (device(g, m_up), 3), (device(g, m_down), 2),
        (device(g_up, m), 5), (device(g_down, m), 4),
    ]
    m_diagonal = (1 - core) * (m_down + 1) + core * (m_up - 1)
    near = [peer for peer, _ in sides] + [device(g, m_core), device(g, m_diagonal)]
    for peer in near:
        pl.semaphore_signal(barrier, inc=1, device_id=peer, device_id_type=MESH)

    def normalise(k):
        rows = pl.ds(pl.multiple_of(k * NORM, NORM), NORM)
        x = s_in[rows, :].astype(F32)
        rs = lax.rsqrt(jnp.sum(x * x, axis=-1, keepdims=True) + EPS)
        u = (x * rs).astype(BF16)
        slots[0, rows, 0:DS] = u
        lhs[rows, 0:DS] = u
        scale[rows, :] = rs
        y = t_in[rows, :].astype(F32)
        ts = lax.rsqrt(jnp.sum(y * y, axis=-1, keepdims=True) + EPS)
        v = (y * ts).astype(BF16)
        slots[0, rows, DS:DU] = v
        lhs[rows, DS:DU] = -v

    flows = [
        (0, 2, xor_peer), (2, 3, x_other), (3, 4, device(g, m_z)), (3 + role, 5, device(g, m_core)),
    ]

    def block_copy(flow, k, short):
        src, dst, to = flows[flow]
        if short:
            rows = pl.ds(pl.multiple_of(k * SHORT, SHORT), SHORT)
        else:
            rows = pl.ds(pl.multiple_of(k * CHUNK - HEAD * (CHUNK - SHORT), CHUNK), CHUNK)
        return pltpu.make_async_remote_copy(
            src_ref=slots.at[src, rows], dst_ref=slots.at[dst, rows],
            send_sem=send.at[flow, k], recv_sem=recv.at[flow, k],
            device_id=to, device_id_type=MESH,
        )

    def w_copy(flow):
        src, dst, to = (flows + [(0, 1, device(g, m_core)), (0, 6, n_peer)])[flow]
        return pltpu.make_async_remote_copy(
            src_ref=wbuf.at[src], dst_ref=wbuf.at[dst],
            send_sem=wsend.at[flow], recv_sem=wrecv.at[flow],
            device_id=to, device_id_type=MESH,
        )

    def to_core(third):
        rows = pl.ds(pl.multiple_of(third * THIRD, THIRD), THIRD)
        return pltpu.make_async_remote_copy(
            src_ref=slots.at[0, rows], dst_ref=slots.at[1, rows],
            send_sem=xsend.at[third], recv_sem=xrecv.at[third],
            device_id=device(g, m_core), device_id_type=MESH,
        )

    n_peer = device(g, x_hi * m_up + (1 - x_hi) * m_diagonal)
    n_sends = x_hi + (1 - x_hi) * (1 - core)
    n_takes = x_hi + (1 - x_hi) * core
    mix = 6 * n_takes + (1 - n_takes)

    def to_mix(third):
        rows = pl.ds(third * THIRD, THIRD)
        return pltpu.make_async_remote_copy(
            src_ref=slots.at[0, rows], dst_ref=slots.at[6, rows],
            send_sem=nsend.at[third], recv_sem=nrecv.at[third],
            device_id=n_peer, device_id_type=MESH,
        )

    columns = [2 - 2 * core, 4 + 0 * core, 3 - 2 * x_hi, 1 + 2 * x_hi, 2 * core]

    def switch_of(slot):
        return plan_in[0, 0, columns[slot - 1]].astype(F32)

    per_norm = NORM // CHUNK
    for part, (low, high) in enumerate(PARTS):
        copies[2 * part].wait()
        copies[2 * part + 1].wait()
        if part == 0:
            normalise(0)
            for copy in small:
                copy.wait()
            for third in range(3):
                row = c_in[pl.ds(third * THIRD, THIRD)].astype(F32).reshape(1, THIRD)
                wbuf[0, third] = jnp.broadcast_to(row, (8, THIRD))
            for i in range(2):
                wbuf[0, 3 + i] = jnp.full((8, THIRD), switch_of(4 + i), F32)
            pl.semaphore_wait(barrier, len(near))
            w_copy(0).start()
            w_copy(4).start()

            @pl.when(n_sends == 1)
            def _():
                w_copy(5).start()

            for k in range(HEAD or per_norm):
                block_copy(0, k, HEAD > 0).start()
        else:
            @pl.loop(low // NORM, high // NORM)
            def _(n):
                normalise(n)
                for i in range(per_norm):
                    block_copy(0, n * per_norm + i + EXTRA, False).start()

        if part >= 1:
            to_core(part - 1).start()

            @pl.when(n_sends == 1)
            def _():
                to_mix(part - 1).start()

    for third in range(3):
        wide = jnp.broadcast_to(wbuf[0, third, 0:1], (THIRD, THIRD))
        wcol[pl.ds(third * THIRD, THIRD), :] = wide.T
    acc[...] = jnp.zeros_like(acc)
    lossacc[...] = jnp.zeros_like(lossacc)

    switches[0] = jnp.float32(1.0)
    for slot in range(5):
        switches[slot + 1] = switch_of(slot + 1)
    w_copy(4).wait_recv()

    def piece(pair, third):
        rows = pl.ds(pl.multiple_of(third * THIRD, THIRD), THIRD)
        both = jnp.concatenate([slots[2 * pair, rows, :], slots[2 * pair + 1, rows, :]], axis=0)
        diff = lax.dot_general(
            lhs[...], both, (((1,), (1,)), ((), ())), preferred_element_type=F32
        )
        w_j = jnp.concatenate(
            [wbuf[2 * pair + b, third] * switches[2 * pair + b] for b in range(2)], axis=1
        )[0:1]
        w_i = wcol[...]
        weighted = jnp.concatenate([w_i, w_i], axis=1) * w_j * diff
        if pair < 2:
            loss = weighted * diff
            lossacc[...] += jnp.sum(loss.reshape(ROWS // 8, 8, 2 * THIRD), axis=0)
        coef[...] = weighted.astype(BF16)

    def gradient(pair, third):
        rows = pl.ds(pl.multiple_of(third * THIRD, THIRD), THIRD)
        both = jnp.concatenate(
            [slots[2 * pair, rows, 0:DS], slots[2 * pair + 1, rows, 0:DS]], axis=0
        )
        acc[...] += jnp.dot(coef[...], both, preferred_element_type=F32)

    def mixed(i0, i1, j0, j1):
        left, right = pl.ds(i0 * THIRD, (i1 - i0) * THIRD), pl.ds(j0 * THIRD, (j1 - j0) * THIRD)
        nt = (((1,), (1,)), ((), ()))
        diff = lax.dot_general(
            slots[mix, left, 0:DS], slots[3, right, 0:DS], nt, preferred_element_type=F32
        ) - lax.dot_general(
            slots[mix, left, DS:DU], slots[3, right, DS:DU], nt, preferred_element_type=F32
        )
        w_j = jnp.concatenate([wbuf[3, j] for j in range(j0, j1)], axis=1)[0:1]
        w_i = jnp.concatenate([mixcol[left, :]] * (j1 - j0), axis=1)
        loss = w_i * w_j * diff * diff
        width = (j1 - j0) * THIRD
        lossacc[:, 0:width] += jnp.sum(loss.reshape((i1 - i0) * THIRD // 8, 8, width), axis=0)

    def signal_sides():
        for peer, place in sides:
            pl.semaphore_signal(tokens.at[place], inc=1, device_id=peer, device_id_type=MESH)

    def wait_sides():
        for place in range(6):
            pl.semaphore_wait(tokens.at[place], 1)

    def partial_sums():
        total_w = jnp.zeros((8, THIRD), F32)
        own_w = jnp.zeros((8, THIRD), F32)
        for third in range(3):
            own_w = own_w + wbuf[0, third]
            for slot in range(6):
                total_w = total_w + wbuf[slot, third] * switches[slot]
        weight_lanes = total_w * jnp.sum(own_w, axis=-1, keepdims=True)
        loss_lanes = jnp.sum(lossacc[:, 0:THIRD] + lossacc[:, THIRD:], axis=0, keepdims=True)
        row_id = lax.broadcasted_iota(jnp.int32, (8, THIRD), 0)
        return jnp.where(row_id == 0, jnp.broadcast_to(loss_lanes, (8, THIRD)), weight_lanes)

    y = g // 2
    z = m // 4
    n_y, n_z = n_group // 2, n_member // 4

    def plane_peer(dh, dl, dy):
        member = m + 2 * (lax.rem(x_hi + dh, 2) - x_hi)
        group = g + (lax.rem(x_lo + dl, 2) - x_lo) + 2 * (lax.rem(y + dy, n_y) - y)
        return device(group, member)

    def around(d, n):
        return min(d, n - d)

    plane = sorted(
        (o for o in itertools.product(range(2), range(2), range(n_y)) if any(o)),
        key=lambda o: (-(2 * o[0] + o[1] - 2 * o[0] * o[1] + around(o[2], n_y)), o),
    )
    ring = sorted(range(1, n_z), key=lambda d: (-around(d, n_z), d))
    rounds = [
        (core, [device(g, m_core)]),
        ((x_hi * 2 + x_lo) * n_y + y, [plane_peer(*o) for o in plane]),
        (z, [device(g, lax.rem(m + 4 * d, n_member)) for d in ring]),
    ]

    def send_round(r, value):
        place, peers = rounds[r]
        tiles[r, place] = value
        for peer in peers:
            pltpu.make_async_remote_copy(
                src_ref=tiles.at[r, place], dst_ref=tiles.at[r, place],
                send_sem=ar_send.at[r], recv_sem=ar_recv.at[r],
                device_id=peer, device_id_type=MESH,
            ).start()

    def all_of(r, sems):
        seen = tiles.at[r, pl.ds(0, len(rounds[r][1]))]
        return pltpu.make_async_copy(seen, seen, sems.at[r])

    def finish_round(r):
        all_of(r, ar_recv).wait()
        total = tiles[r, 0]
        for d in range(1, len(rounds[r][1]) + 1):
            total = total + tiles[r, d]
        return total

    def pass_on(k, short):
        if short:
            active = lambda i: (i >= 0) & (i < HEAD)
        else:
            active = lambda i: (i >= HEAD) & (i < NC)
        for flow, lag in enumerate((0, LAG_Q, LAG_R, LAG_F)):
            @pl.when(active(k - lag))
            def _():
                block_copy(flow, k - lag, short).wait_recv()
                if flow < 3:
                    block_copy(flow + 1, k - lag, short).start()

    def products(k):
        @pl.when((k >= 3) & (k < 3 + TOKENS))
        def _():
            wait_sides()

        @pl.when((k >= 2) & (k < 2 + TOKENS))
        def _():
            signal_sides()

        @pl.when((k < 2 * EARLY) & (lax.rem(k, 2) == 0))
        def _():
            to_core(k // 2).wait_recv()
            piece(0, k // 2)
            gradient(0, k // 2)

        for pair, lag in ((1, LAG_Q), (2, LAG_F)):
            late = k - lag - (FIRST - 1)

            @pl.when((late >= 0) & (lax.rem(late + 3 * PER_THIRD, PER_THIRD) == 0) & (k < STEPS - 1))
            def _():
                piece(pair, late // PER_THIRD)
                if pair == 2:
                    gradient(pair, late // PER_THIRD)
                else:
                    @pl.when(k < LOSS_STEP)
                    def _():
                        gradient(pair, late // PER_THIRD)

        @pl.when(k == LOSS_STEP - PER_THIRD)
        def _():
            @pl.when(n_takes == 1)
            def _():
                w_copy(5).wait_recv()
                to_mix(0).wait_recv()
                to_mix(1).wait_recv()

            factor = 2.0 * wbuf[mix, 4 - x_hi][0:1]
            for third in range(3):
                wide = jnp.broadcast_to(wbuf[mix, third][0:1] * factor, (THIRD, THIRD))
                mixcol[pl.ds(third * THIRD, THIRD), :] = wide.T
            mixed(0, 2, 0, 2)

        @pl.when(k == LOSS_STEP - 1)
        def _():
            @pl.when(n_takes == 1)
            def _():
                to_mix(2).wait_recv()

            mixed(2, 3, 0, 2)

        @pl.when(k == LOSS_STEP)
        def _():
            mixed(0, 3, 2, 3)
            send_round(0, partial_sums())
            gradient(1, 2)

        @pl.when(k == LOSS_STEP + 1)
        def _():
            send_round(1, finish_round(0))

    @pl.loop(0, STEPS)
    def _(k):
        if HEAD:
            @pl.when(k < HEAD + LAG_F)
            def _():
                pass_on(k, True)

        pass_on(k, False)

        for flow, lag in enumerate((0, LAG_Q, LAG_R, LAG_F)):
            @pl.when(k == lag)
            def _():
                w_copy(flow).wait_recv()
                if flow < 3:
                    w_copy(flow + 1).start()

        products(k)

    send_round(2, finish_round(1))
    piece(2, 2)
    gradient(2, 2)

    @pl.loop(0, ROWS // NORM)
    def _(k):
        rows = pl.ds(pl.multiple_of(k * NORM, NORM), NORM)
        u = slots[0, rows, 0:DS].astype(F32)
        a = acc[rows, :]
        along = jnp.sum(a * u, axis=-1, keepdims=True)
        out_buf[rows, :] = (4.0 * scale[rows, :]) * (a - along * u)

    out_copy = pltpu.make_async_copy(out_buf, grad_hbm, out_sem)
    out_copy.start()

    for low, high in ((0, HEAD), (HEAD, NC)) if HEAD else ((0, NC),):
        @pl.loop(low, high)
        def _(k):
            for flow in range(4):
                block_copy(flow, k, high == HEAD).wait_send()

    for third in range(3):
        to_core(third).wait_send()
    for flow in range(5):
        w_copy(flow).wait_send()

    @pl.when(n_sends == 1)
    def _():
        w_copy(5).wait_send()
        for third in range(3):
            to_mix(third).wait_send()

    for r in range(2):
        all_of(r, ar_send).wait()
    out_copy.wait()

    tile = finish_round(2)
    sums = jnp.sum(tile, axis=-1, keepdims=True)
    loss_ref[...] = DS * sums[0:1] / sums[1:2]
    all_of(2, ar_send).wait()


def per_device(student, teacher, counts, plan):
    n_group = lax.axis_size("group")
    n_member = lax.axis_size("member")
    any_space = pl.BlockSpec(memory_space=pl.ANY)
    hbm = pl.BlockSpec(memory_space=pltpu.HBM)
    vmem = pl.BlockSpec(memory_space=pltpu.VMEM)
    dma = pltpu.SemaphoreType.DMA
    grad, loss = pl.pallas_call(
        functools.partial(kernel, n_group, n_member),
        out_shape=(
            jax.ShapeDtypeStruct((ROWS, DS), F32),
            jax.ShapeDtypeStruct((1, 1), F32),
        ),
        in_specs=[hbm, hbm, hbm, hbm],
        out_specs=(any_space, vmem),
        scratch_shapes=[
            pltpu.VMEM((ROWS, DS), BF16),
            pltpu.VMEM((ROWS, DT), BF16),
            pltpu.VMEM((ROWS,), jnp.int32),
            pltpu.SMEM((1, 1, 5), jnp.int32),
            pltpu.SMEM((6,), F32),
            pltpu.VMEM((7, ROWS, DU), BF16),
            pltpu.VMEM((ROWS, DU), BF16),
            pltpu.VMEM((ROWS, DS), F32),
            pltpu.VMEM((ROWS, 2 * THIRD), BF16),
            pltpu.VMEM((ROWS, 1), F32),
            pltpu.VMEM((ROWS, THIRD), F32),
            pltpu.VMEM((ROWS, THIRD), F32),
            pltpu.VMEM((7, 5, 8, THIRD), F32),
            pltpu.VMEM((8, 2 * THIRD), F32),
            pltpu.VMEM((3, 16, 8, THIRD), F32),
            pltpu.VMEM((ROWS, DS), F32),
            dma((3, 4)),
            dma((4, NC)),
            dma((4, NC)),
            dma((3,)),
            dma((3,)),
            dma((3,)),
            dma((3,)),
            dma((6,)),
            dma((6,)),
            dma((3,)),
            dma((3,)),
            dma,
            pltpu.SemaphoreType.REGULAR((6,)),
        ],
        compiler_params=pltpu.CompilerParams(
            collective_id=0, has_side_effects=True, vmem_limit_bytes=48 * 1024 * 1024
        ),
    )(*(pltpu.with_memory_space_constraint(a, pltpu.HBM) for a in (student, teacher, counts, plan)))
    return grad, loss.reshape(())


def solution(mesh):
    return jax.shard_map(
        per_device,
        mesh=mesh,
        in_specs=(
            P(("group", "member"), None),
            P(("group", "member"), None),
            P(("group", "member")),
            P("group", "member", None),
        ),
        out_specs=(P(("group", "member"), None), P()),
        check_vma=False,
    )
```

```python
import functools
import itertools

import jax
import jax.numpy as jnp
from jax import lax
from jax.experimental import pallas as pl
from jax.experimental.pallas import tpu as pltpu
from jax.sharding import PartitionSpec as P

EPS = 1e-06
MESH = pl.DeviceIdType.MESH
ROWS = 384
DS = 768
DT = 1024
DU = DS + DT
THIRD = 128
CHUNK = 16
SHORT = 8
HEAD = 0
EXTRA = HEAD - HEAD * SHORT // CHUNK
NC = ROWS // CHUNK + EXTRA
PER_THIRD = THIRD // CHUNK
FIRST = NC - 2 * PER_THIRD
LAG_Q, LAG_R, LAG_F = 4, 8, 10
STEPS = NC + LAG_F
EARLY = 3
LOSS_STEP = LAG_Q + NC - 1
TOKENS = 8
NORM = 32
PARTS = ((0, NORM), (NORM, THIRD), (THIRD, 2 * THIRD), (2 * THIRD, ROWS))
F32 = jnp.float32
BF16 = jnp.bfloat16


def kernel(
    n_group, n_member,
    s_hbm, t_hbm, c_hbm, plan_hbm,
    grad_hbm, loss_ref,
    s_in, t_in, c_in, plan_in, switches, slots, lhs, acc, coef, scale, wcol, mixcol, wbuf, lossacc, tiles, out_buf,
    in_sem, send, recv, xsend, xrecv, nsend, nrecv, wsend, wrecv, ar_send, ar_recv, out_sem, tokens,
):
    g = lax.axis_index("group")
    m = lax.axis_index("member")
    core = lax.rem(m, 2)
    x_hi = lax.rem(m // 2, 2)
    x_lo = lax.rem(g, 2)
    g_xor = g + 1 - 2 * x_lo
    m_core = m + 1 - 2 * core
    m_xhi = m + 2 - 4 * x_hi
    m_up = lax.rem(m + 4, n_member)
    m_down = lax.rem(m - 4 + n_member, n_member)
    m_z = lax.rem(m + 4 - 8 * x_hi + n_member, n_member)
    g_up = lax.rem(g + 2, n_group)
    g_down = lax.rem(g - 2 + n_group, n_group)
    role = lax.rem(x_hi + core, 2)

    def device(group, member):
        return {"group": group, "member": member}

    small = [
        pltpu.make_async_copy(c_hbm, c_in, in_sem.at[2, 0]),
        pltpu.make_async_copy(plan_hbm, plan_in, in_sem.at[2, 1]),
    ]
    copies = []
    for part, (low, high) in enumerate(PARTS):
        rows = pl.ds(low, high - low)
        for which, (src, dst) in enumerate(((s_hbm, s_in), (t_hbm, t_in))):
            copies.append(pltpu.make_async_copy(src.at[rows], dst.at[rows], in_sem.at[which, part]))
    for copy in copies[:2] + small + copies[2:]:
        copy.start()

    barrier = pltpu.get_barrier_semaphore()
    xor_peer = device(g_xor, m)
    x_other = device(g_xor, m_xhi)
    sides = [
        (xor_peer, 0), (x_other, 1),
        (device(g, m_up), 3), (device(g, m_down), 2),
        (device(g_up, m), 5), (device(g_down, m), 4),
    ]
    m_diagonal = (1 - core) * (m_down + 1) + core * (m_up - 1)
    near = [peer for peer, _ in sides] + [device(g, m_core), device(g, m_diagonal)]
    for peer in near:
        pl.semaphore_signal(barrier, inc=1, device_id=peer, device_id_type=MESH)

    def normalise(k):
        rows = pl.ds(pl.multiple_of(k * NORM, NORM), NORM)
        x = s_in[rows, :].astype(F32)
        rs = lax.rsqrt(jnp.sum(x * x, axis=-1, keepdims=True) + EPS)
        u = (x * rs).astype(BF16)
        slots[0, rows, 0:DS] = u
        lhs[rows, 0:DS] = u
        scale[rows, :] = rs
        y = t_in[rows, :].astype(F32)
        ts = lax.rsqrt(jnp.sum(y * y, axis=-1, keepdims=True) + EPS)
        v = (y * ts).astype(BF16)
        slots[0, rows, DS:DU] = v
        lhs[rows, DS:DU] = -v

    flows = [
        (0, 2, xor_peer), (2, 3, x_other), (3, 4, device(g, m_z)), (3 + role, 5, device(g, m_core)),
    ]

    def block_copy(flow, k, short):
        src, dst, to = flows[flow]
        if short:
            rows = pl.ds(pl.multiple_of(k * SHORT, SHORT), SHORT)
        else:
            rows = pl.ds(pl.multiple_of(k * CHUNK - HEAD * (CHUNK - SHORT), CHUNK), CHUNK)
        return pltpu.make_async_remote_copy(
            src_ref=slots.at[src, rows], dst_ref=slots.at[dst, rows],
            send_sem=send.at[flow, k], recv_sem=recv.at[flow, k],
            device_id=to, device_id_type=MESH,
        )

    def w_copy(flow):
        src, dst, to = (flows + [(0, 1, device(g, m_core)), (0, 6, n_peer)])[flow]
        return pltpu.make_async_remote_copy(
            src_ref=wbuf.at[src], dst_ref=wbuf.at[dst],
            send_sem=wsend.at[flow], recv_sem=wrecv.at[flow],
            device_id=to, device_id_type=MESH,
        )

    def to_core(third):
        rows = pl.ds(pl.multiple_of(third * THIRD, THIRD), THIRD)
        return pltpu.make_async_remote_copy(
            src_ref=slots.at[0, rows], dst_ref=slots.at[1, rows],
            send_sem=xsend.at[third], recv_sem=xrecv.at[third],
            device_id=device(g, m_core), device_id_type=MESH,
        )

    n_peer = device(g, x_hi * m_up + (1 - x_hi) * m_diagonal)
    n_sends = x_hi + (1 - x_hi) * (1 - core)
    n_takes = x_hi + (1 - x_hi) * core
    mix = 6 * n_takes + (1 - n_takes)

    def to_mix(third):
        rows = pl.ds(third * THIRD, THIRD)
        return pltpu.make_async_remote_copy(
            src_ref=slots.at[0, rows], dst_ref=slots.at[6, rows],
            send_sem=nsend.at[third], recv_sem=nrecv.at[third],
            device_id=n_peer, device_id_type=MESH,
        )

    columns = [2 - 2 * core, 4 + 0 * core, 3 - 2 * x_hi, 1 + 2 * x_hi, 2 * core]

    def switch_of(slot):
        return plan_in[0, 0, columns[slot - 1]].astype(F32)

    per_norm = NORM // CHUNK
    for part, (low, high) in enumerate(PARTS):
        copies[2 * part].wait()
        copies[2 * part + 1].wait()
        if part == 0:
            normalise(0)
            for copy in small:
                copy.wait()
            for third in range(3):
                row = c_in[pl.ds(third * THIRD, THIRD)].astype(F32).reshape(1, THIRD)
                wbuf[0, third] = jnp.broadcast_to(row, (8, THIRD))
            for i in range(2):
                wbuf[0, 3 + i] = jnp.full((8, THIRD), switch_of(4 + i), F32)
            pl.semaphore_wait(barrier, len(near))
            w_copy(0).start()
            w_copy(4).start()

            @pl.when(n_sends == 1)
            def _():
                w_copy(5).start()

            for k in range(HEAD or per_norm):
                block_copy(0, k, HEAD > 0).start()
        else:
            @pl.loop(low // NORM, high // NORM)
            def _(n):
                normalise(n)
                for i in range(per_norm):
                    block_copy(0, n * per_norm + i + EXTRA, False).start()

        if part >= 1:
            to_core(part - 1).start()

            @pl.when(n_sends == 1)
            def _():
                to_mix(part - 1).start()

    for third in range(3):
        wide = jnp.broadcast_to(wbuf[0, third, 0:1], (THIRD, THIRD))
        wcol[pl.ds(third * THIRD, THIRD), :] = wide.T
    acc[...] = jnp.zeros_like(acc)
    lossacc[...] = jnp.zeros_like(lossacc)

    switches[0] = jnp.float32(1.0)
    for slot in range(5):
        switches[slot + 1] = switch_of(slot + 1)
    w_copy(4).wait_recv()

    def piece(pair, third):
        rows = pl.ds(pl.multiple_of(third * THIRD, THIRD), THIRD)
        both = jnp.concatenate([slots[2 * pair, rows, :], slots[2 * pair + 1, rows, :]], axis=0)
        diff = lax.dot_general(
            lhs[...], both, (((1,), (1,)), ((), ())), preferred_element_type=F32
        )
        w_j = jnp.concatenate(
            [wbuf[2 * pair + b, third] * switches[2 * pair + b] for b in range(2)], axis=1
        )[0:1]
        w_i = wcol[...]
        weighted = jnp.concatenate([w_i, w_i], axis=1) * w_j * diff
        counted = jnp.where(pair == 2, 0.0, 1.0)
        loss = weighted * diff
        lossacc[...] += counted * jnp.sum(loss.reshape(ROWS // 8, 8, 2 * THIRD), axis=0)
        coef[...] = weighted.astype(BF16)

    def gradient(pair, third):
        rows = pl.ds(pl.multiple_of(third * THIRD, THIRD), THIRD)
        both = jnp.concatenate(
            [slots[2 * pair, rows, 0:DS], slots[2 * pair + 1, rows, 0:DS]], axis=0
        )
        acc[...] += jnp.dot(coef[...], both, preferred_element_type=F32)

    def mixed(third):
        right = pl.ds(pl.multiple_of(third * THIRD, THIRD), THIRD)
        nt = (((1,), (1,)), ((), ()))
        diff = lax.dot_general(
            slots[mix, :, 0:DS], slots[3, right, 0:DS], nt, preferred_element_type=F32
        ) - lax.dot_general(
            slots[mix, :, DS:DU], slots[3, right, DS:DU], nt, preferred_element_type=F32
        )
        loss = mixcol[...] * wbuf[3, third][0:1] * diff * diff
        lossacc[:, 0:THIRD] += jnp.sum(loss.reshape(ROWS // 8, 8, THIRD), axis=0)

    def planned(k):
        first = (k >= 0) & (k < 2 * EARLY) & (lax.rem(k + 2, 2) == 0)
        active = jnp.where(first, 1, 0)
        pair = 0
        third = active * (k // 2)
        for p, lag in ((1, LAG_Q), (2, LAG_F)):
            late = jnp.maximum(k - (lag + FIRST - 1), 0)
            due = (k >= lag + FIRST - 1) & (lax.rem(late, PER_THIRD) == 0) & (late < 3 * PER_THIRD)
            due = jnp.where(due, 1, 0)
            active = active + due
            pair = pair + p * due
            third = third + due * (late // PER_THIRD)
        return active == 1, pair, third

    def signal_sides():
        for peer, place in sides:
            pl.semaphore_signal(tokens.at[place], inc=1, device_id=peer, device_id_type=MESH)

    def wait_sides():
        for place in range(6):
            pl.semaphore_wait(tokens.at[place], 1)

    def partial_sums():
        total_w = jnp.zeros((8, THIRD), F32)
        own_w = jnp.zeros((8, THIRD), F32)
        for third in range(3):
            own_w = own_w + wbuf[0, third]
            for slot in range(6):
                total_w = total_w + wbuf[slot, third] * switches[slot]
        weight_lanes = total_w * jnp.sum(own_w, axis=-1, keepdims=True)
        loss_lanes = jnp.sum(lossacc[:, 0:THIRD] + lossacc[:, THIRD:], axis=0, keepdims=True)
        row_id = lax.broadcasted_iota(jnp.int32, (8, THIRD), 0)
        return jnp.where(row_id == 0, jnp.broadcast_to(loss_lanes, (8, THIRD)), weight_lanes)

    y = g // 2
    z = m // 4
    n_y, n_z = n_group // 2, n_member // 4

    def plane_peer(dh, dl, dy):
        member = m + 2 * (lax.rem(x_hi + dh, 2) - x_hi)
        group = g + (lax.rem(x_lo + dl, 2) - x_lo) + 2 * (lax.rem(y + dy, n_y) - y)
        return device(group, member)

    def around(d, n):
        return min(d, n - d)

    plane = sorted(
        (o for o in itertools.product(range(2), range(2), range(n_y)) if any(o)),
        key=lambda o: (-(2 * o[0] + o[1] - 2 * o[0] * o[1] + around(o[2], n_y)), o),
    )
    ring = sorted(range(1, n_z), key=lambda d: (-around(d, n_z), d))
    rounds = [
        (core, [device(g, m_core)]),
        ((x_hi * 2 + x_lo) * n_y + y, [plane_peer(*o) for o in plane]),
        (z, [device(g, lax.rem(m + 4 * d, n_member)) for d in ring]),
    ]

    def send_round(r, value):
        place, peers = rounds[r]
        tiles[r, place] = value
        for peer in peers:
            pltpu.make_async_remote_copy(
                src_ref=tiles.at[r, place], dst_ref=tiles.at[r, place],
                send_sem=ar_send.at[r], recv_sem=ar_recv.at[r],
                device_id=peer, device_id_type=MESH,
            ).start()

    def all_of(r, sems):
        seen = tiles.at[r, pl.ds(0, len(rounds[r][1]))]
        return pltpu.make_async_copy(seen, seen, sems.at[r])

    def finish_round(r):
        all_of(r, ar_recv).wait()
        total = tiles[r, 0]
        for d in range(1, len(rounds[r][1]) + 1):
            total = total + tiles[r, d]
        return total

    def pass_on(k, short):
        if short:
            active = lambda i: (i >= 0) & (i < HEAD)
        else:
            active = lambda i: (i >= HEAD) & (i < NC)
        for flow, lag in enumerate((0, LAG_Q, LAG_R, LAG_F)):
            @pl.when(active(k - lag))
            def _():
                block_copy(flow, k - lag, short).wait_recv()
                if flow < 3:
                    block_copy(flow + 1, k - lag, short).start()

    def products(k):
        @pl.when((k >= 4) & (k < 4 + 2 * TOKENS) & (lax.rem(k, 2) == 0))
        def _():
            wait_sides()

        @pl.when((k >= 2) & (k < 2 + 2 * TOKENS) & (lax.rem(k, 2) == 0))
        def _():
            signal_sides()

        @pl.when(k == LOSS_STEP - PER_THIRD)
        def _():
            @pl.when(n_takes == 1)
            def _():
                w_copy(5).wait_recv()

            factor = 2.0 * wbuf[mix, 4 - x_hi][0:1]
            for third in range(3):
                wide = jnp.broadcast_to(wbuf[mix, third][0:1] * factor, (THIRD, THIRD))
                mixcol[pl.ds(third * THIRD, THIRD), :] = wide.T

        @pl.when((k == LOSS_STEP - 3) & (n_takes == 1))
        def _():
            for third in range(3):
                to_mix(third).wait_recv()

        @pl.when(k == LOSS_STEP + 1)
        def _():
            send_round(1, finish_round(0))

        @pl.when(k == NC + LAG_R)
        def _():
            send_round(2, finish_round(1))

        @pl.when((k < 2 * EARLY) & (lax.rem(k, 2) == 0))
        def _():
            to_core(k // 2).wait_recv()

        before, pair_before, third_before = planned(k - 1)

        @pl.when(before)
        def _():
            gradient(pair_before, third_before)

        now, pair_now, third_now = planned(k)

        @pl.when(now)
        def _():
            piece(pair_now, third_now)

        @pl.when((k == LOSS_STEP - 3) | (k == LOSS_STEP - 1) | (k == LOSS_STEP))
        def _():
            mixed(jnp.maximum(k - (LOSS_STEP - 2), 0))

        @pl.when(k == LOSS_STEP)
        def _():
            send_round(0, partial_sums())

    @pl.loop(0, STEPS + 1)
    def _(k):
        if HEAD:
            @pl.when(k < HEAD + LAG_F)
            def _():
                pass_on(k, True)

        pass_on(k, False)

        for flow, lag in enumerate((0, LAG_Q, LAG_R, LAG_F)):
            @pl.when(k == lag)
            def _():
                w_copy(flow).wait_recv()
                if flow < 3:
                    w_copy(flow + 1).start()

        products(k)

    @pl.loop(0, ROWS // NORM)
    def _(k):
        rows = pl.ds(pl.multiple_of(k * NORM, NORM), NORM)
        u = slots[0, rows, 0:DS].astype(F32)
        a = acc[rows, :]
        along = jnp.sum(a * u, axis=-1, keepdims=True)
        out_buf[rows, :] = (4.0 * scale[rows, :]) * (a - along * u)

    out_copy = pltpu.make_async_copy(out_buf, grad_hbm, out_sem)
    out_copy.start()

    for low, high in ((0, HEAD), (HEAD, NC)) if HEAD else ((0, NC),):
        @pl.loop(low, high)
        def _(k):
            for flow in range(4):
                block_copy(flow, k, high == HEAD).wait_send()

    for third in range(3):
        to_core(third).wait_send()
    for flow in range(5):
        w_copy(flow).wait_send()

    @pl.when(n_sends == 1)
    def _():
        w_copy(5).wait_send()
        for third in range(3):
            to_mix(third).wait_send()

    for r in range(2):
        all_of(r, ar_send).wait()
    out_copy.wait()

    tile = finish_round(2)
    sums = jnp.sum(tile, axis=-1, keepdims=True)
    loss_ref[...] = DS * sums[0:1] / sums[1:2]
    all_of(2, ar_send).wait()


def per_device(student, teacher, counts, plan):
    n_group = lax.axis_size("group")
    n_member = lax.axis_size("member")
    any_space = pl.BlockSpec(memory_space=pl.ANY)
    hbm = pl.BlockSpec(memory_space=pltpu.HBM)
    vmem = pl.BlockSpec(memory_space=pltpu.VMEM)
    dma = pltpu.SemaphoreType.DMA
    grad, loss = pl.pallas_call(
        functools.partial(kernel, n_group, n_member),
        out_shape=(
            jax.ShapeDtypeStruct((ROWS, DS), F32),
            jax.ShapeDtypeStruct((1, 1), F32),
        ),
        in_specs=[hbm, hbm, hbm, hbm],
        out_specs=(any_space, vmem),
        scratch_shapes=[
            pltpu.VMEM((ROWS, DS), BF16),
            pltpu.VMEM((ROWS, DT), BF16),
            pltpu.VMEM((ROWS,), jnp.int32),
            pltpu.SMEM((1, 1, 5), jnp.int32),
            pltpu.SMEM((6,), F32),
            pltpu.VMEM((7, ROWS, DU), BF16),
            pltpu.VMEM((ROWS, DU), BF16),
            pltpu.VMEM((ROWS, DS), F32),
            pltpu.VMEM((ROWS, 2 * THIRD), BF16),
            pltpu.VMEM((ROWS, 1), F32),
            pltpu.VMEM((ROWS, THIRD), F32),
            pltpu.VMEM((ROWS, THIRD), F32),
            pltpu.VMEM((7, 5, 8, THIRD), F32),
            pltpu.VMEM((8, 2 * THIRD), F32),
            pltpu.VMEM((3, 16, 8, THIRD), F32),
            pltpu.VMEM((ROWS, DS), F32),
            dma((3, 4)),
            dma((4, NC)),
            dma((4, NC)),
            dma((3,)),
            dma((3,)),
            dma((3,)),
            dma((3,)),
            dma((6,)),
            dma((6,)),
            dma((3,)),
            dma((3,)),
            dma,
            pltpu.SemaphoreType.REGULAR((6,)),
        ],
        compiler_params=pltpu.CompilerParams(
            collective_id=0, has_side_effects=True, vmem_limit_bytes=48 * 1024 * 1024
        ),
    )(*(pltpu.with_memory_space_constraint(a, pltpu.HBM) for a in (student, teacher, counts, plan)))
    return grad, loss.reshape(())


def solution(mesh):
    return jax.shard_map(
        per_device,
        mesh=mesh,
        in_specs=(
            P(("group", "member"), None),
            P(("group", "member"), None),
            P(("group", "member")),
            P("group", "member", None),
        ),
        out_specs=(P(("group", "member"), None), P()),
        check_vma=False,
    )
```

```python
import functools
import itertools

import jax
import jax.numpy as jnp
from jax import lax
from jax.experimental import pallas as pl
from jax.experimental.pallas import tpu as pltpu
from jax.sharding import PartitionSpec as P

EPS = 1e-06
MESH = pl.DeviceIdType.MESH
ROWS = 384
DS = 768
DT = 1024
DU = DS + DT
THIRD = 128
CHUNK = 16
SHORT = 8
HEAD = 0
EXTRA = HEAD - HEAD * SHORT // CHUNK
NC = ROWS // CHUNK + EXTRA
PER_THIRD = THIRD // CHUNK
FIRST = NC - 2 * PER_THIRD
LAG_Q, LAG_R, LAG_F = 3, 7, 9
STEPS = NC + LAG_F
EARLY = 3
LOSS_STEP = LAG_Q + NC - 1
Z_STEP = LOSS_STEP + 3
TOKENS = 8
NORM = 32
PARTS = ((0, NORM), (NORM, THIRD), (THIRD, 2 * THIRD), (2 * THIRD, ROWS))
F32 = jnp.float32
BF16 = jnp.bfloat16


def kernel(
    n_group, n_member,
    s_hbm, t_hbm, c_hbm, plan_hbm,
    grad_hbm, loss_ref,
    s_in, t_in, c_in, plan_in, switches, slots, lhs, acc, coef, scale, wcol, mixcol, wbuf, lossacc, tiles, out_buf,
    in_sem, send, recv, xsend, xrecv, nsend, nrecv, wsend, wrecv, ar_send, ar_recv, out_sem, tokens,
):
    g = lax.axis_index("group")
    m = lax.axis_index("member")
    core = lax.rem(m, 2)
    x_hi = lax.rem(m // 2, 2)
    x_lo = lax.rem(g, 2)
    g_xor = g + 1 - 2 * x_lo
    m_core = m + 1 - 2 * core
    m_xhi = m + 2 - 4 * x_hi
    m_up = lax.rem(m + 4, n_member)
    m_down = lax.rem(m - 4 + n_member, n_member)
    m_z = lax.rem(m + 4 - 8 * x_hi + n_member, n_member)
    g_up = lax.rem(g + 2, n_group)
    g_down = lax.rem(g - 2 + n_group, n_group)
    role = lax.rem(x_hi + core, 2)

    def device(group, member):
        return {"group": group, "member": member}

    small = [
        pltpu.make_async_copy(c_hbm, c_in, in_sem.at[2, 0]),
        pltpu.make_async_copy(plan_hbm, plan_in, in_sem.at[2, 1]),
    ]
    copies = []
    for part, (low, high) in enumerate(PARTS):
        rows = pl.ds(low, high - low)
        for which, (src, dst) in enumerate(((s_hbm, s_in), (t_hbm, t_in))):
            copies.append(pltpu.make_async_copy(src.at[rows], dst.at[rows], in_sem.at[which, part]))
    for copy in copies[:2] + small + copies[2:]:
        copy.start()

    barrier = pltpu.get_barrier_semaphore()
    xor_peer = device(g_xor, m)
    x_other = device(g_xor, m_xhi)
    sides = [
        (xor_peer, 0), (x_other, 1),
        (device(g, m_up), 3), (device(g, m_down), 2),
        (device(g_up, m), 5), (device(g_down, m), 4),
    ]
    m_diagonal = (1 - core) * (m_down + 1) + core * (m_up - 1)
    near = [peer for peer, _ in sides] + [device(g, m_core), device(g, m_diagonal)]
    for peer in near:
        pl.semaphore_signal(barrier, inc=1, device_id=peer, device_id_type=MESH)

    def normalise(k):
        rows = pl.ds(pl.multiple_of(k * NORM, NORM), NORM)
        x = s_in[rows, :].astype(F32)
        rs = lax.rsqrt(jnp.sum(x * x, axis=-1, keepdims=True) + EPS)
        u = (x * rs).astype(BF16)
        slots[0, rows, 0:DS] = u
        lhs[rows, 0:DS] = u
        scale[rows, :] = rs
        y = t_in[rows, :].astype(F32)
        ts = lax.rsqrt(jnp.sum(y * y, axis=-1, keepdims=True) + EPS)
        v = (y * ts).astype(BF16)
        slots[0, rows, DS:DU] = v
        lhs[rows, DS:DU] = -v

    flows = [
        (0, 2, xor_peer), (2, 3, x_other), (3, 4, device(g, m_z)), (3 + role, 5, device(g, m_core)),
    ]

    def block_copy(flow, k, short):
        src, dst, to = flows[flow]
        if short:
            rows = pl.ds(pl.multiple_of(k * SHORT, SHORT), SHORT)
        else:
            rows = pl.ds(pl.multiple_of(k * CHUNK - HEAD * (CHUNK - SHORT), CHUNK), CHUNK)
        return pltpu.make_async_remote_copy(
            src_ref=slots.at[src, rows], dst_ref=slots.at[dst, rows],
            send_sem=send.at[flow, k], recv_sem=recv.at[flow, k],
            device_id=to, device_id_type=MESH,
        )

    def w_copy(flow):
        src, dst, to = (flows + [(0, 1, device(g, m_core)), (0, 6, n_peer)])[flow]
        return pltpu.make_async_remote_copy(
            src_ref=wbuf.at[src], dst_ref=wbuf.at[dst],
            send_sem=wsend.at[flow], recv_sem=wrecv.at[flow],
            device_id=to, device_id_type=MESH,
        )

    def to_core(third):
        rows = pl.ds(pl.multiple_of(third * THIRD, THIRD), THIRD)
        return pltpu.make_async_remote_copy(
            src_ref=slots.at[0, rows], dst_ref=slots.at[1, rows],
            send_sem=xsend.at[third], recv_sem=xrecv.at[third],
            device_id=device(g, m_core), device_id_type=MESH,
        )

    n_peer = device(g, x_hi * m_up + (1 - x_hi) * m_diagonal)
    n_sends = x_hi + (1 - x_hi) * (1 - core)
    n_takes = x_hi + (1 - x_hi) * core
    mix = 6 * n_takes + (1 - n_takes)

    def to_mix(third):
        rows = pl.ds(third * THIRD, THIRD)
        return pltpu.make_async_remote_copy(
            src_ref=slots.at[0, rows], dst_ref=slots.at[6, rows],
            send_sem=nsend.at[third], recv_sem=nrecv.at[third],
            device_id=n_peer, device_id_type=MESH,
        )

    columns = [2 - 2 * core, 4 + 0 * core, 3 - 2 * x_hi, 1 + 2 * x_hi, 2 * core]

    def switch_of(slot):
        return plan_in[0, 0, columns[slot - 1]].astype(F32)

    per_norm = NORM // CHUNK
    for part, (low, high) in enumerate(PARTS):
        copies[2 * part].wait()
        copies[2 * part + 1].wait()
        if part == 0:
            normalise(0)
            for copy in small:
                copy.wait()
            for third in range(3):
                row = c_in[pl.ds(third * THIRD, THIRD)].astype(F32).reshape(1, THIRD)
                wbuf[0, third] = jnp.broadcast_to(row, (8, THIRD))
            for i in range(2):
                wbuf[0, 3 + i] = jnp.full((8, THIRD), switch_of(4 + i), F32)
            pl.semaphore_wait(barrier, len(near))
            w_copy(0).start()
            w_copy(4).start()

            @pl.when(n_sends == 1)
            def _():
                w_copy(5).start()

            for k in range(HEAD or per_norm):
                block_copy(0, k, HEAD > 0).start()
        else:
            @pl.loop(low // NORM, high // NORM)
            def _(n):
                normalise(n)
                for i in range(per_norm):
                    block_copy(0, n * per_norm + i + EXTRA, False).start()

        if part >= 1:
            to_core(part - 1).start()

            @pl.when(n_sends == 1)
            def _():
                to_mix(part - 1).start()

    for third in range(3):
        wide = jnp.broadcast_to(wbuf[0, third, 0:1], (THIRD, THIRD))
        wcol[pl.ds(third * THIRD, THIRD), :] = wide.T
    acc[...] = jnp.zeros_like(acc)
    lossacc[...] = jnp.zeros_like(lossacc)

    switches[0] = jnp.float32(1.0)
    for slot in range(5):
        switches[slot + 1] = switch_of(slot + 1)
    w_copy(4).wait_recv()

    def piece(pair, third):
        rows = pl.ds(pl.multiple_of(third * THIRD, THIRD), THIRD)
        both = jnp.concatenate([slots[2 * pair, rows, :], slots[2 * pair + 1, rows, :]], axis=0)
        diff = lax.dot_general(
            lhs[...], both, (((1,), (1,)), ((), ())), preferred_element_type=F32
        )
        w_j = jnp.concatenate(
            [wbuf[2 * pair + b, third] * switches[2 * pair + b] for b in range(2)], axis=1
        )[0:1]
        w_i = wcol[...]
        weighted = jnp.concatenate([w_i, w_i], axis=1) * w_j * diff
        counted = jnp.where(pair == 2, 0.0, 1.0)
        loss = weighted * diff
        lossacc[...] += counted * jnp.sum(loss.reshape(ROWS // 8, 8, 2 * THIRD), axis=0)
        coef[...] = weighted.astype(BF16)

    def gradient(pair, third):
        rows = pl.ds(pl.multiple_of(third * THIRD, THIRD), THIRD)
        both = jnp.concatenate(
            [slots[2 * pair, rows, 0:DS], slots[2 * pair + 1, rows, 0:DS]], axis=0
        )
        acc[...] += jnp.dot(coef[...], both, preferred_element_type=F32)

    def mixed(third):
        right = pl.ds(pl.multiple_of(third * THIRD, THIRD), THIRD)
        nt = (((1,), (1,)), ((), ()))
        diff = lax.dot_general(
            slots[mix, :, 0:DS], slots[3, right, 0:DS], nt, preferred_element_type=F32
        ) - lax.dot_general(
            slots[mix, :, DS:DU], slots[3, right, DS:DU], nt, preferred_element_type=F32
        )
        loss = mixcol[...] * wbuf[3, third][0:1] * diff * diff
        lossacc[:, 0:THIRD] += jnp.sum(loss.reshape(ROWS // 8, 8, THIRD), axis=0)

    def planned(k):
        first = (k >= 0) & (k < 2 * EARLY) & (lax.rem(k + 2, 2) == 0)
        active = jnp.where(first, 1, 0)
        pair = 0
        third = active * (k // 2)
        for p, lag in ((1, LAG_Q), (2, LAG_F)):
            late = jnp.maximum(k - (lag + FIRST - 1), 0)
            due = (k >= lag + FIRST - 1) & (lax.rem(late, PER_THIRD) == 0) & (late < 3 * PER_THIRD)
            due = jnp.where(due, 1, 0)
            active = active + due
            pair = pair + p * due
            third = third + due * (late // PER_THIRD)
        return active == 1, pair, third

    def signal_sides():
        for peer, place in sides:
            pl.semaphore_signal(tokens.at[place], inc=1, device_id=peer, device_id_type=MESH)

    def wait_sides():
        for place in range(6):
            pl.semaphore_wait(tokens.at[place], 1)

    def partial_sums():
        total_w = jnp.zeros((8, THIRD), F32)
        own_w = jnp.zeros((8, THIRD), F32)
        for third in range(3):
            own_w = own_w + wbuf[0, third]
            for slot in range(6):
                total_w = total_w + wbuf[slot, third] * switches[slot]
        weight_lanes = total_w * jnp.sum(own_w, axis=-1, keepdims=True)
        loss_lanes = jnp.sum(lossacc[:, 0:THIRD] + lossacc[:, THIRD:], axis=0, keepdims=True)
        row_id = lax.broadcasted_iota(jnp.int32, (8, THIRD), 0)
        return jnp.where(row_id == 0, jnp.broadcast_to(loss_lanes, (8, THIRD)), weight_lanes)

    y = g // 2
    z = m // 4
    n_y, n_z = n_group // 2, n_member // 4

    def plane_peer(dh, dl, dy):
        member = m + 2 * (lax.rem(x_hi + dh, 2) - x_hi)
        group = g + (lax.rem(x_lo + dl, 2) - x_lo) + 2 * (lax.rem(y + dy, n_y) - y)
        return device(group, member)

    def around(d, n):
        return min(d, n - d)

    plane = sorted(
        (o for o in itertools.product(range(2), range(2), range(n_y)) if any(o)),
        key=lambda o: (-(2 * o[0] + o[1] - 2 * o[0] * o[1] + around(o[2], n_y)), o),
    )
    ring = sorted(range(1, n_z), key=lambda d: (-around(d, n_z), d))
    rounds = [
        (core, [device(g, m_core)]),
        ((x_hi * 2 + x_lo) * n_y + y, [plane_peer(*o) for o in plane]),
        (z, [device(g, lax.rem(m + 4 * d, n_member)) for d in ring]),
    ]

    def send_round(r, value):
        place, peers = rounds[r]
        tiles[r, place] = value
        for peer in peers:
            pltpu.make_async_remote_copy(
                src_ref=tiles.at[r, place], dst_ref=tiles.at[r, place],
                send_sem=ar_send.at[r], recv_sem=ar_recv.at[r],
                device_id=peer, device_id_type=MESH,
            ).start()

    def all_of(r, sems):
        seen = tiles.at[r, pl.ds(0, len(rounds[r][1]))]
        return pltpu.make_async_copy(seen, seen, sems.at[r])

    def finish_round(r):
        all_of(r, ar_recv).wait()
        total = tiles[r, 0]
        for d in range(1, len(rounds[r][1]) + 1):
            total = total + tiles[r, d]
        return total

    def pass_on(k, short):
        if short:
            active = lambda i: (i >= 0) & (i < HEAD)
        else:
            active = lambda i: (i >= HEAD) & (i < NC)
        for flow, lag in enumerate((0, LAG_Q, LAG_R, LAG_F)):
            @pl.when(active(k - lag))
            def _():
                block_copy(flow, k - lag, short).wait_recv()
                if flow < 3:
                    block_copy(flow + 1, k - lag, short).start()

    def products(k):
        @pl.when((k >= 4) & (k < 4 + 2 * TOKENS) & (lax.rem(k, 2) == 0))
        def _():
            wait_sides()

        @pl.when((k >= 2) & (k < 2 + 2 * TOKENS) & (lax.rem(k, 2) == 0))
        def _():
            signal_sides()

        @pl.when(k == LOSS_STEP - PER_THIRD)
        def _():
            @pl.when(n_takes == 1)
            def _():
                w_copy(5).wait_recv()

            factor = 2.0 * wbuf[mix, 4 - x_hi][0:1]
            for third in range(3):
                wide = jnp.broadcast_to(wbuf[mix, third][0:1] * factor, (THIRD, THIRD))
                mixcol[pl.ds(third * THIRD, THIRD), :] = wide.T

        @pl.when((k == LOSS_STEP - 3) & (n_takes == 1))
        def _():
            for third in range(3):
                to_mix(third).wait_recv()

        @pl.when((k < 2 * EARLY) & (lax.rem(k, 2) == 0))
        def _():
            to_core(k // 2).wait_recv()

        before, pair_before, third_before = planned(k - 1)

        @pl.when(before)
        def _():
            gradient(pair_before, third_before)

        now, pair_now, third_now = planned(k)

        @pl.when(now)
        def _():
            piece(pair_now, third_now)

        @pl.when((k == LOSS_STEP - 3) | (k == LOSS_STEP - 1) | (k == LOSS_STEP))
        def _():
            mixed(jnp.maximum(k - (LOSS_STEP - 2), 0))

        @pl.when(k == LOSS_STEP)
        def _():
            send_round(0, partial_sums())

    @pl.loop(0, STEPS + 1)
    def _(k):
        @pl.when(k == LOSS_STEP + 1)
        def _():
            send_round(1, finish_round(0))

        @pl.when(k == Z_STEP)
        def _():
            send_round(2, finish_round(1))

        if HEAD:
            @pl.when(k < HEAD + LAG_F)
            def _():
                pass_on(k, True)

        pass_on(k, False)

        for flow, lag in enumerate((0, LAG_Q, LAG_R, LAG_F)):
            @pl.when(k == lag)
            def _():
                w_copy(flow).wait_recv()
                if flow < 3:
                    w_copy(flow + 1).start()

        products(k)

    @pl.loop(0, ROWS // NORM)
    def _(k):
        rows = pl.ds(pl.multiple_of(k * NORM, NORM), NORM)
        u = slots[0, rows, 0:DS].astype(F32)
        a = acc[rows, :]
        along = jnp.sum(a * u, axis=-1, keepdims=True)
        out_buf[rows, :] = (4.0 * scale[rows, :]) * (a - along * u)

    out_copy = pltpu.make_async_copy(out_buf, grad_hbm, out_sem)
    out_copy.start()

    for low, high in ((0, HEAD), (HEAD, NC)) if HEAD else ((0, NC),):
        @pl.loop(low, high)
        def _(k):
            for flow in range(4):
                block_copy(flow, k, high == HEAD).wait_send()

    for third in range(3):
        to_core(third).wait_send()
    for flow in range(5):
        w_copy(flow).wait_send()

    @pl.when(n_sends == 1)
    def _():
        w_copy(5).wait_send()
        for third in range(3):
            to_mix(third).wait_send()

    for r in range(2):
        all_of(r, ar_send).wait()
    out_copy.wait()

    tile = finish_round(2)
    sums = jnp.sum(tile, axis=-1, keepdims=True)
    loss_ref[...] = DS * sums[0:1] / sums[1:2]
    all_of(2, ar_send).wait()


def per_device(student, teacher, counts, plan):
    n_group = lax.axis_size("group")
    n_member = lax.axis_size("member")
    any_space = pl.BlockSpec(memory_space=pl.ANY)
    hbm = pl.BlockSpec(memory_space=pltpu.HBM)
    vmem = pl.BlockSpec(memory_space=pltpu.VMEM)
    dma = pltpu.SemaphoreType.DMA
    grad, loss = pl.pallas_call(
        functools.partial(kernel, n_group, n_member),
        out_shape=(
            jax.ShapeDtypeStruct((ROWS, DS), F32),
            jax.ShapeDtypeStruct((1, 1), F32),
        ),
        in_specs=[hbm, hbm, hbm, hbm],
        out_specs=(any_space, vmem),
        scratch_shapes=[
            pltpu.VMEM((ROWS, DS), BF16),
            pltpu.VMEM((ROWS, DT), BF16),
            pltpu.VMEM((ROWS,), jnp.int32),
            pltpu.SMEM((1, 1, 5), jnp.int32),
            pltpu.SMEM((6,), F32),
            pltpu.VMEM((7, ROWS, DU), BF16),
            pltpu.VMEM((ROWS, DU), BF16),
            pltpu.VMEM((ROWS, DS), F32),
            pltpu.VMEM((ROWS, 2 * THIRD), BF16),
            pltpu.VMEM((ROWS, 1), F32),
            pltpu.VMEM((ROWS, THIRD), F32),
            pltpu.VMEM((ROWS, THIRD), F32),
            pltpu.VMEM((7, 5, 8, THIRD), F32),
            pltpu.VMEM((8, 2 * THIRD), F32),
            pltpu.VMEM((3, 16, 8, THIRD), F32),
            pltpu.VMEM((ROWS, DS), F32),
            dma((3, 4)),
            dma((4, NC)),
            dma((4, NC)),
            dma((3,)),
            dma((3,)),
            dma((3,)),
            dma((3,)),
            dma((6,)),
            dma((6,)),
            dma((3,)),
            dma((3,)),
            dma,
            pltpu.SemaphoreType.REGULAR((6,)),
        ],
        compiler_params=pltpu.CompilerParams(
            collective_id=0, has_side_effects=True, vmem_limit_bytes=48 * 1024 * 1024
        ),
    )(*(pltpu.with_memory_space_constraint(a, pltpu.HBM) for a in (student, teacher, counts, plan)))
    return grad, loss.reshape(())


def solution(mesh):
    return jax.shard_map(
        per_device,
        mesh=mesh,
        in_specs=(
            P(("group", "member"), None),
            P(("group", "member"), None),
            P(("group", "member")),
            P("group", "member", None),
        ),
        out_specs=(P(("group", "member"), None), P()),
        check_vma=False,
    )
```

```python
import functools
import itertools

import jax
import jax.numpy as jnp
from jax import lax
from jax.experimental import pallas as pl
from jax.experimental.pallas import tpu as pltpu
from jax.sharding import PartitionSpec as P

EPS = 1e-06
MESH = pl.DeviceIdType.MESH
ROWS = 384
DS = 768
DT = 1024
DU = DS + DT
THIRD = 128
CHUNK = 16
SHORT = 8
HEAD = 0
EXTRA = HEAD - HEAD * SHORT // CHUNK
NC = ROWS // CHUNK + EXTRA
PER_THIRD = THIRD // CHUNK
FIRST = NC - 2 * PER_THIRD
LAG_Q, LAG_R, LAG_F = 3, 7, 9
STEPS = NC + LAG_F
EARLY = 3
LOSS_STEP = LAG_Q + NC - 1
Z_STEP = LOSS_STEP + 2
TOKENS = 8
NORM = 32
PARTS = ((0, NORM), (NORM, THIRD), (THIRD, 2 * THIRD), (2 * THIRD, ROWS))
F32 = jnp.float32
BF16 = jnp.bfloat16


def kernel(
    n_group, n_member,
    s_hbm, t_hbm, c_hbm, plan_hbm,
    grad_hbm, loss_ref,
    s_in, t_in, c_in, plan_in, switches, slots, lhs, acc, coef, scale, wcol, mixcol, wbuf, lossacc, tiles, out_buf,
    in_sem, send, recv, xsend, xrecv, nsend, nrecv, wsend, wrecv, ar_send, ar_recv, out_sem, tokens,
):
    g = lax.axis_index("group")
    m = lax.axis_index("member")
    core = lax.rem(m, 2)
    x_hi = lax.rem(m // 2, 2)
    x_lo = lax.rem(g, 2)
    g_xor = g + 1 - 2 * x_lo
    m_core = m + 1 - 2 * core
    m_xhi = m + 2 - 4 * x_hi
    m_up = lax.rem(m + 4, n_member)
    m_down = lax.rem(m - 4 + n_member, n_member)
    m_z = lax.rem(m + 4 - 8 * x_hi + n_member, n_member)
    g_up = lax.rem(g + 2, n_group)
    g_down = lax.rem(g - 2 + n_group, n_group)
    role = lax.rem(x_hi + core, 2)

    def device(group, member):
        return {"group": group, "member": member}

    small = [
        pltpu.make_async_copy(c_hbm, c_in, in_sem.at[2, 0]),
        pltpu.make_async_copy(plan_hbm, plan_in, in_sem.at[2, 1]),
    ]
    copies = []
    for part, (low, high) in enumerate(PARTS):
        rows = pl.ds(low, high - low)
        for which, (src, dst) in enumerate(((s_hbm, s_in), (t_hbm, t_in))):
            copies.append(pltpu.make_async_copy(src.at[rows], dst.at[rows], in_sem.at[which, part]))
    for copy in copies[:2]:
        copy.start()

    barrier = pltpu.get_barrier_semaphore()
    xor_peer = device(g_xor, m)
    x_other = device(g_xor, m_xhi)
    sides = [
        (xor_peer, 0), (x_other, 1),
        (device(g, m_up), 3), (device(g, m_down), 2),
        (device(g_up, m), 5), (device(g_down, m), 4),
    ]
    m_diagonal = (1 - core) * (m_down + 1) + core * (m_up - 1)
    near = [peer for peer, _ in sides] + [device(g, m_core), device(g, m_diagonal)]
    for peer in near:
        pl.semaphore_signal(barrier, inc=1, device_id=peer, device_id_type=MESH)
    for copy in small + copies[2:]:
        copy.start()

    def normalise(k):
        rows = pl.ds(pl.multiple_of(k * NORM, NORM), NORM)
        x = s_in[rows, :].astype(F32)
        rs = lax.rsqrt(jnp.sum(x * x, axis=-1, keepdims=True) + EPS)
        u = (x * rs).astype(BF16)
        slots[0, rows, 0:DS] = u
        lhs[rows, 0:DS] = u
        scale[rows, :] = rs
        y = t_in[rows, :].astype(F32)
        ts = lax.rsqrt(jnp.sum(y * y, axis=-1, keepdims=True) + EPS)
        v = (y * ts).astype(BF16)
        slots[0, rows, DS:DU] = v
        lhs[rows, DS:DU] = -v

    flows = [
        (0, 2, xor_peer), (2, 3, x_other), (3, 4, device(g, m_z)), (3 + role, 5, device(g, m_core)),
    ]

    def block_copy(flow, k, short):
        src, dst, to = flows[flow]
        if short:
            rows = pl.ds(pl.multiple_of(k * SHORT, SHORT), SHORT)
        else:
            rows = pl.ds(pl.multiple_of(k * CHUNK - HEAD * (CHUNK - SHORT), CHUNK), CHUNK)
        return pltpu.make_async_remote_copy(
            src_ref=slots.at[src, rows], dst_ref=slots.at[dst, rows],
            send_sem=send.at[flow, k], recv_sem=recv.at[flow, k],
            device_id=to, device_id_type=MESH,
        )

    def w_copy(flow):
        src, dst, to = (flows + [(0, 1, device(g, m_core)), (0, 6, n_peer)])[flow]
        return pltpu.make_async_remote_copy(
            src_ref=wbuf.at[src], dst_ref=wbuf.at[dst],
            send_sem=wsend.at[flow], recv_sem=wrecv.at[flow],
            device_id=to, device_id_type=MESH,
        )

    def to_core(third):
        rows = pl.ds(pl.multiple_of(third * THIRD, THIRD), THIRD)
        return pltpu.make_async_remote_copy(
            src_ref=slots.at[0, rows], dst_ref=slots.at[1, rows],
            send_sem=xsend.at[third], recv_sem=xrecv.at[third],
            device_id=device(g, m_core), device_id_type=MESH,
        )

    n_peer = device(g, x_hi * m_up + (1 - x_hi) * m_diagonal)
    n_sends = x_hi + (1 - x_hi) * (1 - core)
    n_takes = x_hi + (1 - x_hi) * core
    mix = 6 * n_takes + (1 - n_takes)

    def to_mix(third):
        rows = pl.ds(third * THIRD, THIRD)
        return pltpu.make_async_remote_copy(
            src_ref=slots.at[0, rows], dst_ref=slots.at[6, rows],
            send_sem=nsend.at[third], recv_sem=nrecv.at[third],
            device_id=n_peer, device_id_type=MESH,
        )

    columns = [2 - 2 * core, 4 + 0 * core, 3 - 2 * x_hi, 1 + 2 * x_hi, 2 * core]

    def switch_of(slot):
        return plan_in[0, 0, columns[slot - 1]].astype(F32)

    per_norm = NORM // CHUNK
    for part, (low, high) in enumerate(PARTS):
        copies[2 * part].wait()
        copies[2 * part + 1].wait()
        if part == 0:
            normalise(0)
            for copy in small:
                copy.wait()
            for third in range(3):
                row = c_in[pl.ds(third * THIRD, THIRD)].astype(F32).reshape(1, THIRD)
                wbuf[0, third] = jnp.broadcast_to(row, (8, THIRD))
            for i in range(2):
                wbuf[0, 3 + i] = jnp.full((8, THIRD), switch_of(4 + i), F32)
            pl.semaphore_wait(barrier, len(near))
            w_copy(0).start()
            w_copy(4).start()

            @pl.when(n_sends == 1)
            def _():
                w_copy(5).start()

            for k in range(HEAD or per_norm):
                block_copy(0, k, HEAD > 0).start()
        else:
            @pl.loop(low // NORM, high // NORM)
            def _(n):
                normalise(n)
                for i in range(per_norm):
                    block_copy(0, n * per_norm + i + EXTRA, False).start()

        if part >= 1:
            to_core(part - 1).start()

            @pl.when(n_sends == 1)
            def _():
                to_mix(part - 1).start()

    for third in range(3):
        wide = jnp.broadcast_to(wbuf[0, third, 0:1], (THIRD, THIRD))
        wcol[pl.ds(third * THIRD, THIRD), :] = wide.T
    acc[...] = jnp.zeros_like(acc)
    lossacc[...] = jnp.zeros_like(lossacc)

    switches[0] = jnp.float32(1.0)
    for slot in range(5):
        switches[slot + 1] = switch_of(slot + 1)
    w_copy(4).wait_recv()

    def piece(pair, third):
        rows = pl.ds(pl.multiple_of(third * THIRD, THIRD), THIRD)
        both = jnp.concatenate([slots[2 * pair, rows, :], slots[2 * pair + 1, rows, :]], axis=0)
        diff = lax.dot_general(
            lhs[...], both, (((1,), (1,)), ((), ())), preferred_element_type=F32
        )
        w_j = jnp.concatenate(
            [wbuf[2 * pair + b, third] * switches[2 * pair + b] for b in range(2)], axis=1
        )[0:1]
        w_i = wcol[...]
        weighted = jnp.concatenate([w_i, w_i], axis=1) * w_j * diff
        counted = jnp.where(pair == 2, 0.0, 1.0)
        loss = weighted * diff
        lossacc[...] += counted * jnp.sum(loss.reshape(ROWS // 8, 8, 2 * THIRD), axis=0)
        coef[...] = weighted.astype(BF16)

    def gradient(pair, third):
        rows = pl.ds(pl.multiple_of(third * THIRD, THIRD), THIRD)
        both = jnp.concatenate(
            [slots[2 * pair, rows, 0:DS], slots[2 * pair + 1, rows, 0:DS]], axis=0
        )
        acc[...] += jnp.dot(coef[...], both, preferred_element_type=F32)

    def mixed(third):
        right = pl.ds(pl.multiple_of(third * THIRD, THIRD), THIRD)
        nt = (((1,), (1,)), ((), ()))
        diff = lax.dot_general(
            slots[mix, :, 0:DS], slots[3, right, 0:DS], nt, preferred_element_type=F32
        ) - lax.dot_general(
            slots[mix, :, DS:DU], slots[3, right, DS:DU], nt, preferred_element_type=F32
        )
        loss = mixcol[...] * wbuf[3, third][0:1] * diff * diff
        lossacc[:, 0:THIRD] += jnp.sum(loss.reshape(ROWS // 8, 8, THIRD), axis=0)

    def planned(k):
        first = (k >= 0) & (k < 2 * EARLY) & (lax.rem(k + 2, 2) == 0)
        active = jnp.where(first, 1, 0)
        pair = 0
        third = active * (k // 2)
        for p, lag in ((1, LAG_Q), (2, LAG_F)):
            late = jnp.maximum(k - (lag + FIRST - 1), 0)
            due = (k >= lag + FIRST - 1) & (lax.rem(late, PER_THIRD) == 0) & (late < 3 * PER_THIRD)
            due = jnp.where(due, 1, 0)
            active = active + due
            pair = pair + p * due
            third = third + due * (late // PER_THIRD)
        return active == 1, pair, third

    def signal_sides():
        for peer, place in sides:
            pl.semaphore_signal(tokens.at[place], inc=1, device_id=peer, device_id_type=MESH)

    def wait_sides():
        for place in range(6):
            pl.semaphore_wait(tokens.at[place], 1)

    def partial_sums():
        total_w = jnp.zeros((8, THIRD), F32)
        own_w = jnp.zeros((8, THIRD), F32)
        for third in range(3):
            own_w = own_w + wbuf[0, third]
            for slot in range(6):
                total_w = total_w + wbuf[slot, third] * switches[slot]
        weight_lanes = total_w * jnp.sum(own_w, axis=-1, keepdims=True)
        loss_lanes = jnp.sum(lossacc[:, 0:THIRD] + lossacc[:, THIRD:], axis=0, keepdims=True)
        row_id = lax.broadcasted_iota(jnp.int32, (8, THIRD), 0)
        return jnp.where(row_id == 0, jnp.broadcast_to(loss_lanes, (8, THIRD)), weight_lanes)

    y = g // 2
    z = m // 4
    n_y, n_z = n_group // 2, n_member // 4

    def plane_peer(dh, dl, dy):
        member = m + 2 * (lax.rem(x_hi + dh, 2) - x_hi)
        group = g + (lax.rem(x_lo + dl, 2) - x_lo) + 2 * (lax.rem(y + dy, n_y) - y)
        return device(group, member)

    def around(d, n):
        return min(d, n - d)

    plane = sorted(
        (o for o in itertools.product(range(2), range(2), range(n_y)) if any(o)),
        key=lambda o: (-(2 * o[0] + o[1] - 2 * o[0] * o[1] + around(o[2], n_y)), o),
    )
    ring = sorted(range(1, n_z), key=lambda d: (-around(d, n_z), d))
    rounds = [
        (core, [device(g, m_core)]),
        ((x_hi * 2 + x_lo) * n_y + y, [plane_peer(*o) for o in plane]),
        (z, [device(g, lax.rem(m + 4 * d, n_member)) for d in ring]),
    ]

    def send_round(r, value):
        place, peers = rounds[r]
        tiles[r, place] = value
        for peer in peers:
            pltpu.make_async_remote_copy(
                src_ref=tiles.at[r, place], dst_ref=tiles.at[r, place],
                send_sem=ar_send.at[r], recv_sem=ar_recv.at[r],
                device_id=peer, device_id_type=MESH,
            ).start()

    def all_of(r, sems):
        seen = tiles.at[r, pl.ds(0, len(rounds[r][1]))]
        return pltpu.make_async_copy(seen, seen, sems.at[r])

    def finish_round(r):
        all_of(r, ar_recv).wait()
        total = tiles[r, 0]
        for d in range(1, len(rounds[r][1]) + 1):
            total = total + tiles[r, d]
        return total

    def pass_on(k, short):
        if short:
            active = lambda i: (i >= 0) & (i < HEAD)
        else:
            active = lambda i: (i >= HEAD) & (i < NC)
        for flow, lag in enumerate((0, LAG_Q, LAG_R, LAG_F)):
            @pl.when(active(k - lag))
            def _():
                block_copy(flow, k - lag, short).wait_recv()
                if flow < 3:
                    block_copy(flow + 1, k - lag, short).start()

    def products(k):
        @pl.when((k >= 4) & (k < 4 + 2 * TOKENS) & (lax.rem(k, 2) == 0))
        def _():
            wait_sides()

        @pl.when((k >= 2) & (k < 2 + 2 * TOKENS) & (lax.rem(k, 2) == 0))
        def _():
            signal_sides()

        @pl.when(k == LOSS_STEP - PER_THIRD)
        def _():
            @pl.when(n_takes == 1)
            def _():
                w_copy(5).wait_recv()

            factor = 2.0 * wbuf[mix, 4 - x_hi][0:1]
            for third in range(3):
                wide = jnp.broadcast_to(wbuf[mix, third][0:1] * factor, (THIRD, THIRD))
                mixcol[pl.ds(third * THIRD, THIRD), :] = wide.T

        @pl.when((k == LOSS_STEP - 3) & (n_takes == 1))
        def _():
            for third in range(3):
                to_mix(third).wait_recv()

        @pl.when((k < 2 * EARLY) & (lax.rem(k, 2) == 0))
        def _():
            to_core(k // 2).wait_recv()

        before, pair_before, third_before = planned(k - 1)

        @pl.when(before)
        def _():
            gradient(pair_before, third_before)

        now, pair_now, third_now = planned(k)

        @pl.when(now)
        def _():
            piece(pair_now, third_now)

        @pl.when((k == LOSS_STEP - 3) | (k == LOSS_STEP - 1) | (k == LOSS_STEP))
        def _():
            mixed(jnp.maximum(k - (LOSS_STEP - 2), 0))

        @pl.when(k == LOSS_STEP)
        def _():
            send_round(0, partial_sums())

    @pl.loop(0, STEPS + 1)
    def _(k):
        @pl.when(k == LOSS_STEP + 1)
        def _():
            send_round(1, finish_round(0))

        @pl.when(k == Z_STEP)
        def _():
            send_round(2, finish_round(1))

        if HEAD:
            @pl.when(k < HEAD + LAG_F)
            def _():
                pass_on(k, True)

        pass_on(k, False)

        for flow, lag in enumerate((0, LAG_Q, LAG_R, LAG_F)):
            @pl.when(k == lag)
            def _():
                w_copy(flow).wait_recv()
                if flow < 3:
                    w_copy(flow + 1).start()

        products(k)

    @pl.loop(0, ROWS // NORM)
    def _(k):
        rows = pl.ds(pl.multiple_of(k * NORM, NORM), NORM)
        u = slots[0, rows, 0:DS].astype(F32)
        a = acc[rows, :]
        along = jnp.sum(a * u, axis=-1, keepdims=True)
        out_buf[rows, :] = (4.0 * scale[rows, :]) * (a - along * u)

    out_copy = pltpu.make_async_copy(out_buf, grad_hbm, out_sem)
    out_copy.start()

    for low, high in ((0, HEAD), (HEAD, NC)) if HEAD else ((0, NC),):
        @pl.loop(low, high)
        def _(k):
            for flow in range(4):
                block_copy(flow, k, high == HEAD).wait_send()

    for third in range(3):
        to_core(third).wait_send()
    for flow in range(5):
        w_copy(flow).wait_send()

    @pl.when(n_sends == 1)
    def _():
        w_copy(5).wait_send()
        for third in range(3):
            to_mix(third).wait_send()

    for r in range(2):
        all_of(r, ar_send).wait()
    out_copy.wait()

    tile = finish_round(2)
    sums = jnp.sum(tile, axis=-1, keepdims=True)
    loss_ref[...] = DS * sums[0:1] / sums[1:2]
    all_of(2, ar_send).wait()


def per_device(student, teacher, counts, plan):
    n_group = lax.axis_size("group")
    n_member = lax.axis_size("member")
    any_space = pl.BlockSpec(memory_space=pl.ANY)
    hbm = pl.BlockSpec(memory_space=pltpu.HBM)
    vmem = pl.BlockSpec(memory_space=pltpu.VMEM)
    dma = pltpu.SemaphoreType.DMA
    grad, loss = pl.pallas_call(
        functools.partial(kernel, n_group, n_member),
        out_shape=(
            jax.ShapeDtypeStruct((ROWS, DS), F32),
            jax.ShapeDtypeStruct((1, 1), F32),
        ),
        in_specs=[hbm, hbm, hbm, hbm],
        out_specs=(any_space, vmem),
        scratch_shapes=[
            pltpu.VMEM((ROWS, DS), BF16),
            pltpu.VMEM((ROWS, DT), BF16),
            pltpu.VMEM((ROWS,), jnp.int32),
            pltpu.SMEM((1, 1, 5), jnp.int32),
            pltpu.SMEM((6,), F32),
            pltpu.VMEM((7, ROWS, DU), BF16),
            pltpu.VMEM((ROWS, DU), BF16),
            pltpu.VMEM((ROWS, DS), F32),
            pltpu.VMEM((ROWS, 2 * THIRD), BF16),
            pltpu.VMEM((ROWS, 1), F32),
            pltpu.VMEM((ROWS, THIRD), F32),
            pltpu.VMEM((ROWS, THIRD), F32),
            pltpu.VMEM((7, 5, 8, THIRD), F32),
            pltpu.VMEM((8, 2 * THIRD), F32),
            pltpu.VMEM((3, 16, 8, THIRD), F32),
            pltpu.VMEM((ROWS, DS), F32),
            dma((3, 4)),
            dma((4, NC)),
            dma((4, NC)),
            dma((3,)),
            dma((3,)),
            dma((3,)),
            dma((3,)),
            dma((6,)),
            dma((6,)),
            dma((3,)),
            dma((3,)),
            dma,
            pltpu.SemaphoreType.REGULAR((6,)),
        ],
        compiler_params=pltpu.CompilerParams(
            collective_id=0, has_side_effects=True, vmem_limit_bytes=48 * 1024 * 1024
        ),
    )(*(pltpu.with_memory_space_constraint(a, pltpu.HBM) for a in (student, teacher, counts, plan)))
    return grad, loss.reshape(())


def solution(mesh):
    return jax.shard_map(
        per_device,
        mesh=mesh,
        in_specs=(
            P(("group", "member"), None),
            P(("group", "member"), None),
            P(("group", "member")),
            P("group", "member", None),
        ),
        out_specs=(P(("group", "member"), None), P()),
        check_vma=False,
    )
```

```python
import functools
import itertools

import jax
import jax.numpy as jnp
from jax import lax
from jax.experimental import pallas as pl
from jax.experimental.pallas import tpu as pltpu
from jax.sharding import PartitionSpec as P

EPS = 1e-06
MESH = pl.DeviceIdType.MESH
ROWS = 384
DS = 768
DT = 1024
DU = DS + DT
THIRD = 128
CHUNK = 16
SHORT = 8
HEAD = 0
EXTRA = HEAD - HEAD * SHORT // CHUNK
NC = ROWS // CHUNK + EXTRA
PER_THIRD = THIRD // CHUNK
FIRST = NC - 2 * PER_THIRD
LAG_Q, LAG_R, LAG_F = 3, 7, 9
STEPS = NC + LAG_F
EARLY = 3
LOSS_STEP = LAG_Q + NC - 1
Z_STEP = LOSS_STEP + 2
TOKENS = 8
NORM = 32
PARTS = ((0, NORM), (NORM, THIRD), (THIRD, 2 * THIRD), (2 * THIRD, ROWS))
F32 = jnp.float32
BF16 = jnp.bfloat16


def kernel(
    n_group, n_member,
    s_hbm, t_hbm, c_hbm, plan_hbm,
    grad_hbm, loss_ref,
    s_in, t_in, c_in, plan_in, switches, slots, lhs, acc, coef, scale, wcol, mixcol, wbuf, lossacc, tiles, out_buf,
    in_sem, send, recv, xsend, xrecv, nsend, nrecv, wsend, wrecv, ar_send, ar_recv, out_sem, tokens,
):
    g = lax.axis_index("group")
    m = lax.axis_index("member")
    core = lax.rem(m, 2)
    x_hi = lax.rem(m // 2, 2)
    x_lo = lax.rem(g, 2)
    g_xor = g + 1 - 2 * x_lo
    m_core = m + 1 - 2 * core
    m_xhi = m + 2 - 4 * x_hi
    m_up = lax.rem(m + 4, n_member)
    m_down = lax.rem(m - 4 + n_member, n_member)
    m_z = lax.rem(m + 4 - 8 * x_hi + n_member, n_member)
    g_up = lax.rem(g + 2, n_group)
    g_down = lax.rem(g - 2 + n_group, n_group)
    role = lax.rem(x_hi + core, 2)

    def device(group, member):
        return {"group": group, "member": member}

    small = [
        pltpu.make_async_copy(c_hbm, c_in, in_sem.at[2, 0]),
        pltpu.make_async_copy(plan_hbm, plan_in, in_sem.at[2, 1]),
    ]
    copies = []
    for part, (low, high) in enumerate(PARTS):
        rows = pl.ds(low, high - low)
        for which, (src, dst) in enumerate(((s_hbm, s_in), (t_hbm, t_in))):
            copies.append(pltpu.make_async_copy(src.at[rows], dst.at[rows], in_sem.at[which, part]))
    for copy in copies[:2] + small + copies[2:]:
        copy.start()

    barrier = pltpu.get_barrier_semaphore()
    xor_peer = device(g_xor, m)
    x_other = device(g_xor, m_xhi)
    sides = [
        (xor_peer, 0), (x_other, 1),
        (device(g, m_up), 3), (device(g, m_down), 2),
        (device(g_up, m), 5), (device(g_down, m), 4),
    ]
    m_diagonal = (1 - core) * (m_down + 1) + core * (m_up - 1)
    near = [peer for peer, _ in sides] + [device(g, m_core), device(g, m_diagonal)]
    for peer in near:
        pl.semaphore_signal(barrier, inc=1, device_id=peer, device_id_type=MESH)

    def normalise(k):
        rows = pl.ds(pl.multiple_of(k * NORM, NORM), NORM)
        x = s_in[rows, :].astype(F32)
        rs = lax.rsqrt(jnp.sum(x * x, axis=-1, keepdims=True) + EPS)
        u = (x * rs).astype(BF16)
        slots[0, rows, 0:DS] = u
        lhs[rows, 0:DS] = u
        scale[rows, :] = rs
        y = t_in[rows, :].astype(F32)
        ts = lax.rsqrt(jnp.sum(y * y, axis=-1, keepdims=True) + EPS)
        v = (y * ts).astype(BF16)
        slots[0, rows, DS:DU] = v
        lhs[rows, DS:DU] = -v

    flows = [
        (0, 2, xor_peer), (2, 3, x_other), (3, 4, device(g, m_z)), (3 + role, 5, device(g, m_core)),
    ]

    def block_copy(flow, k, short):
        src, dst, to = flows[flow]
        if short:
            rows = pl.ds(pl.multiple_of(k * SHORT, SHORT), SHORT)
        else:
            rows = pl.ds(pl.multiple_of(k * CHUNK - HEAD * (CHUNK - SHORT), CHUNK), CHUNK)
        return pltpu.make_async_remote_copy(
            src_ref=slots.at[src, rows], dst_ref=slots.at[dst, rows],
            send_sem=send.at[flow, k], recv_sem=recv.at[flow, k],
            device_id=to, device_id_type=MESH,
        )

    def w_copy(flow):
        src, dst, to = (flows + [(0, 1, device(g, m_core)), (0, 6, n_peer)])[flow]
        return pltpu.make_async_remote_copy(
            src_ref=wbuf.at[src], dst_ref=wbuf.at[dst],
            send_sem=wsend.at[flow], recv_sem=wrecv.at[flow],
            device_id=to, device_id_type=MESH,
        )

    def to_core(third):
        rows = pl.ds(pl.multiple_of(third * THIRD, THIRD), THIRD)
        return pltpu.make_async_remote_copy(
            src_ref=slots.at[0, rows], dst_ref=slots.at[1, rows],
            send_sem=xsend.at[third], recv_sem=xrecv.at[third],
            device_id=device(g, m_core), device_id_type=MESH,
        )

    n_peer = device(g, x_hi * m_up + (1 - x_hi) * m_diagonal)
    n_sends = x_hi + (1 - x_hi) * (1 - core)
    n_takes = x_hi + (1 - x_hi) * core
    mix = 6 * n_takes + (1 - n_takes)

    def to_mix(third):
        rows = pl.ds(third * THIRD, THIRD)
        return pltpu.make_async_remote_copy(
            src_ref=slots.at[0, rows], dst_ref=slots.at[6, rows],
            send_sem=nsend.at[third], recv_sem=nrecv.at[third],
            device_id=n_peer, device_id_type=MESH,
        )

    columns = [2 - 2 * core, 4 + 0 * core, 3 - 2 * x_hi, 1 + 2 * x_hi, 2 * core]

    def switch_of(slot):
        return plan_in[0, 0, columns[slot - 1]].astype(F32)

    per_norm = NORM // CHUNK
    for part, (low, high) in enumerate(PARTS):
        copies[2 * part].wait()
        copies[2 * part + 1].wait()
        if part == 0:
            normalise(0)
            for copy in small:
                copy.wait()
            for third in range(3):
                row = c_in[pl.ds(third * THIRD, THIRD)].astype(F32).reshape(1, THIRD)
                wbuf[0, third] = jnp.broadcast_to(row, (8, THIRD))
            for i in range(2):
                wbuf[0, 3 + i] = jnp.full((8, THIRD), switch_of(4 + i), F32)
            pl.semaphore_wait(barrier, len(near))
            w_copy(0).start()
            w_copy(4).start()

            @pl.when(n_sends == 1)
            def _():
                w_copy(5).start()

            for k in range(HEAD or per_norm):
                block_copy(0, k, HEAD > 0).start()
        else:
            @pl.loop(low // NORM, high // NORM)
            def _(n):
                normalise(n)
                for i in range(per_norm):
                    block_copy(0, n * per_norm + i + EXTRA, False).start()

        if part >= 1:
            to_core(part - 1).start()

            @pl.when(n_sends == 1)
            def _():
                to_mix(part - 1).start()

    for third in range(3):
        wide = jnp.broadcast_to(wbuf[0, third, 0:1], (THIRD, THIRD))
        wcol[pl.ds(third * THIRD, THIRD), :] = wide.T
    acc[...] = jnp.zeros_like(acc)
    lossacc[...] = jnp.zeros_like(lossacc)

    switches[0] = jnp.float32(1.0)
    for slot in range(5):
        switches[slot + 1] = switch_of(slot + 1)
    w_copy(4).wait_recv()

    def piece(pair, third):
        rows = pl.ds(pl.multiple_of(third * THIRD, THIRD), THIRD)
        both = jnp.concatenate([slots[2 * pair, rows, :], slots[2 * pair + 1, rows, :]], axis=0)
        diff = lax.dot_general(
            lhs[...], both, (((1,), (1,)), ((), ())), preferred_element_type=F32
        )
        w_j = jnp.concatenate(
            [wbuf[2 * pair + b, third] * switches[2 * pair + b] for b in range(2)], axis=1
        )[0:1]
        w_i = wcol[...]
        weighted = jnp.concatenate([w_i, w_i], axis=1) * w_j * diff
        counted = jnp.where(pair == 2, 0.0, 1.0)
        loss = weighted * diff
        lossacc[...] += counted * jnp.sum(loss.reshape(ROWS // 8, 8, 2 * THIRD), axis=0)
        coef[...] = weighted.astype(BF16)

    def gradient(pair, third):
        rows = pl.ds(pl.multiple_of(third * THIRD, THIRD), THIRD)
        both = jnp.concatenate(
            [slots[2 * pair, rows, 0:DS], slots[2 * pair + 1, rows, 0:DS]], axis=0
        )
        acc[...] += jnp.dot(coef[...], both, preferred_element_type=F32)

    def mixed(third):
        right = pl.ds(pl.multiple_of(third * THIRD, THIRD), THIRD)
        nt = (((1,), (1,)), ((), ()))
        diff = lax.dot_general(
            slots[mix, :, 0:DS], slots[3, right, 0:DS], nt, preferred_element_type=F32
        ) - lax.dot_general(
            slots[mix, :, DS:DU], slots[3, right, DS:DU], nt, preferred_element_type=F32
        )
        loss = mixcol[...] * wbuf[3, third][0:1] * diff * diff
        lossacc[:, 0:THIRD] += jnp.sum(loss.reshape(ROWS // 8, 8, THIRD), axis=0)

    def planned(k):
        first = (k >= 0) & (k < 2 * EARLY) & (lax.rem(k + 2, 2) == 0)
        active = jnp.where(first, 1, 0)
        pair = 0
        third = active * (k // 2)
        for p, lag in ((1, LAG_Q), (2, LAG_F)):
            late = jnp.maximum(k - (lag + FIRST - 1), 0)
            due = (k >= lag + FIRST - 1) & (lax.rem(late, PER_THIRD) == 0) & (late < 3 * PER_THIRD)
            due = jnp.where(due, 1, 0)
            active = active + due
            pair = pair + p * due
            third = third + due * (late // PER_THIRD)
        return active == 1, pair, third

    def signal_sides():
        for peer, place in sides:
            pl.semaphore_signal(tokens.at[place], inc=1, device_id=peer, device_id_type=MESH)

    def wait_sides():
        for place in range(6):
            pl.semaphore_wait(tokens.at[place], 1)

    def partial_sums():
        total_w = jnp.zeros((8, THIRD), F32)
        own_w = jnp.zeros((8, THIRD), F32)
        for third in range(3):
            own_w = own_w + wbuf[0, third]
            for slot in range(6):
                total_w = total_w + wbuf[slot, third] * switches[slot]
        weight_lanes = total_w * jnp.sum(own_w, axis=-1, keepdims=True)
        loss_lanes = jnp.sum(lossacc[:, 0:THIRD] + lossacc[:, THIRD:], axis=0, keepdims=True)
        row_id = lax.broadcasted_iota(jnp.int32, (8, THIRD), 0)
        return jnp.where(row_id == 0, jnp.broadcast_to(loss_lanes, (8, THIRD)), weight_lanes)

    y = g // 2
    z = m // 4
    n_y, n_z = n_group // 2, n_member // 4

    def plane_peer(dh, dl, dy):
        member = m + 2 * (lax.rem(x_hi + dh, 2) - x_hi)
        group = g + (lax.rem(x_lo + dl, 2) - x_lo) + 2 * (lax.rem(y + dy, n_y) - y)
        return device(group, member)

    def around(d, n):
        return min(d, n - d)

    plane = sorted(
        (o for o in itertools.product(range(2), range(2), range(n_y)) if any(o)),
        key=lambda o: (-(2 * o[0] + o[1] - 2 * o[0] * o[1] + around(o[2], n_y)), o),
    )
    ring = sorted(range(1, n_z), key=lambda d: (-around(d, n_z), d))
    rounds = [
        (core, [device(g, m_core)]),
        ((x_hi * 2 + x_lo) * n_y + y, [plane_peer(*o) for o in plane]),
        (z, [device(g, lax.rem(m + 4 * d, n_member)) for d in ring]),
    ]

    def send_round(r, value):
        place, peers = rounds[r]
        tiles[r, place] = value
        for peer in peers:
            pltpu.make_async_remote_copy(
                src_ref=tiles.at[r, place], dst_ref=tiles.at[r, place],
                send_sem=ar_send.at[r], recv_sem=ar_recv.at[r],
                device_id=peer, device_id_type=MESH,
            ).start()

    def all_of(r, sems):
        seen = tiles.at[r, pl.ds(0, len(rounds[r][1]))]
        return pltpu.make_async_copy(seen, seen, sems.at[r])

    def finish_round(r):
        all_of(r, ar_recv).wait()
        total = tiles[r, 0]
        for d in range(1, len(rounds[r][1]) + 1):
            total = total + tiles[r, d]
        return total

    def pass_on(k, short):
        if short:
            active = lambda i: (i >= 0) & (i < HEAD)
        else:
            active = lambda i: (i >= HEAD) & (i < NC)
        for flow, lag in enumerate((0, LAG_Q, LAG_R, LAG_F)):
            @pl.when(active(k - lag))
            def _():
                block_copy(flow, k - lag, short).wait_recv()
                if flow < 3:
                    block_copy(flow + 1, k - lag, short).start()

    def products(k):
        @pl.when((k >= 4) & (k < 4 + 2 * TOKENS) & (lax.rem(k, 2) == 0))
        def _():
            wait_sides()

        @pl.when((k >= 2) & (k < 2 + 2 * TOKENS) & (lax.rem(k, 2) == 0))
        def _():
            signal_sides()

        @pl.when(k == LOSS_STEP - PER_THIRD)
        def _():
            @pl.when(n_takes == 1)
            def _():
                w_copy(5).wait_recv()

            factor = 2.0 * wbuf[mix, 4 - x_hi][0:1]
            for third in range(3):
                wide = jnp.broadcast_to(wbuf[mix, third][0:1] * factor, (THIRD, THIRD))
                mixcol[pl.ds(third * THIRD, THIRD), :] = wide.T

        @pl.when((k == LOSS_STEP - 3) & (n_takes == 1))
        def _():
            for third in range(3):
                to_mix(third).wait_recv()

        @pl.when((k < 2 * EARLY) & (lax.rem(k, 2) == 0))
        def _():
            to_core(k // 2).wait_recv()

        before, pair_before, third_before = planned(k - 1)

        @pl.when(before)
        def _():
            gradient(pair_before, third_before)

        now, pair_now, third_now = planned(k)

        @pl.when(now)
        def _():
            piece(pair_now, third_now)

        @pl.when((k == LOSS_STEP - 3) | (k == LOSS_STEP - 1) | (k == LOSS_STEP))
        def _():
            mixed(jnp.maximum(k - (LOSS_STEP - 2), 0))

        @pl.when(k == LOSS_STEP)
        def _():
            send_round(0, partial_sums())

    @pl.loop(0, STEPS + 1)
    def _(k):
        @pl.when(k == LOSS_STEP + 1)
        def _():
            send_round(1, finish_round(0))

        @pl.when(k == Z_STEP)
        def _():
            send_round(2, finish_round(1))

        if HEAD:
            @pl.when(k < HEAD + LAG_F)
            def _():
                pass_on(k, True)

        pass_on(k, False)

        for flow, lag in enumerate((0, LAG_Q, LAG_R, LAG_F)):
            @pl.when(k == lag)
            def _():
                w_copy(flow).wait_recv()
                if flow < 3:
                    w_copy(flow + 1).start()

        products(k)

    @pl.loop(0, ROWS // NORM)
    def _(k):
        rows = pl.ds(pl.multiple_of(k * NORM, NORM), NORM)
        u = slots[0, rows, 0:DS].astype(F32)
        a = acc[rows, :]
        along = jnp.sum(a * u, axis=-1, keepdims=True)
        out_buf[rows, :] = (4.0 * scale[rows, :]) * (a - along * u)

    out_copy = pltpu.make_async_copy(out_buf, grad_hbm, out_sem)
    out_copy.start()

    for low, high in ((0, HEAD), (HEAD, NC)) if HEAD else ((0, NC),):
        @pl.loop(low, high)
        def _(k):
            for flow in range(4):
                block_copy(flow, k, high == HEAD).wait_send()

    for third in range(3):
        to_core(third).wait_send()
    for flow in range(5):
        w_copy(flow).wait_send()

    @pl.when(n_sends == 1)
    def _():
        w_copy(5).wait_send()
        for third in range(3):
            to_mix(third).wait_send()

    for r in range(2):
        all_of(r, ar_send).wait()
    out_copy.wait()

    tile = finish_round(2)
    sums = jnp.sum(tile, axis=-1, keepdims=True)
    loss_ref[...] = DS * sums[0:1] / sums[1:2]
    all_of(2, ar_send).wait()


def per_device(student, teacher, counts, plan):
    n_group = lax.axis_size("group")
    n_member = lax.axis_size("member")
    any_space = pl.BlockSpec(memory_space=pl.ANY)
    hbm = pl.BlockSpec(memory_space=pltpu.HBM)
    vmem = pl.BlockSpec(memory_space=pltpu.VMEM)
    dma = pltpu.SemaphoreType.DMA
    grad, loss = pl.pallas_call(
        functools.partial(kernel, n_group, n_member),
        out_shape=(
            jax.ShapeDtypeStruct((ROWS, DS), F32),
            jax.ShapeDtypeStruct((1, 1), F32),
        ),
        in_specs=[hbm, hbm, hbm, hbm],
        out_specs=(any_space, vmem),
        scratch_shapes=[
            pltpu.VMEM((ROWS, DS), BF16),
            pltpu.VMEM((ROWS, DT), BF16),
            pltpu.VMEM((ROWS,), jnp.int32),
            pltpu.SMEM((1, 1, 5), jnp.int32),
            pltpu.SMEM((6,), F32),
            pltpu.VMEM((7, ROWS, DU), BF16),
            pltpu.VMEM((ROWS, DU), BF16),
            pltpu.VMEM((ROWS, DS), F32),
            pltpu.VMEM((ROWS, 2 * THIRD), BF16),
            pltpu.VMEM((ROWS, 1), F32),
            pltpu.VMEM((ROWS, THIRD), F32),
            pltpu.VMEM((ROWS, THIRD), F32),
            pltpu.VMEM((7, 5, 8, THIRD), F32),
            pltpu.VMEM((8, 2 * THIRD), F32),
            pltpu.VMEM((3, 16, 8, THIRD), F32),
            pltpu.VMEM((ROWS, DS), F32),
            dma((3, 4)),
            dma((4, NC)),
            dma((4, NC)),
            dma((3,)),
            dma((3,)),
            dma((3,)),
            dma((3,)),
            dma((6,)),
            dma((6,)),
            dma((3,)),
            dma((3,)),
            dma,
            pltpu.SemaphoreType.REGULAR((6,)),
        ],
        compiler_params=pltpu.CompilerParams(
            collective_id=0, has_side_effects=True, vmem_limit_bytes=48 * 1024 * 1024
        ),
    )(*(pltpu.with_memory_space_constraint(a, pltpu.HBM) for a in (student, teacher, counts, plan)))
    return grad, loss.reshape(())


def solution(mesh):
    return jax.shard_map(
        per_device,
        mesh=mesh,
        in_specs=(
            P(("group", "member"), None),
            P(("group", "member"), None),
            P(("group", "member")),
            P("group", "member", None),
        ),
        out_specs=(P(("group", "member"), None), P()),
        check_vma=False,
    )
```
